32 devices in a mesh: groups: 2 (over y), wide: 4 (over x, core), narrow: 4 (over z).
Axes of the slice: x: 2, y: 2, z: 4, core: 2. Of those that a mesh axis runs over, the one named last changes fastest.
Arguments:
- basis: bfloat16 [128, 64, 2, 512], P(('groups', 'wide'), 'narrow'), parts along dimension 0, may hold values from -0.25 to 0.25
- kappa: float32 [128, 64, 2], P(('groups', 'wide'), 'narrow'), parts along dimension 0, may hold values from 0.1 to 1
- velocity: float32 [3, 512], P(None, 'groups'), parts along dimension 1, may hold values from -2 to 2
- coefficients: float32 [512, 512], P('groups'), parts along dimension 0, may hold values from -6 to 6
- propagator: float32 [1024, 512], P('groups'), parts along dimension 0, may hold values from -0.25 to 0.25
Outputs:
- advanced: float32 [512, 512], P(('groups', 'wide', 'narrow')), parts along dimension 0
The draws below stay inside these ranges and needn't reach their ends.
There are 2 independent parts, one for each index of `groups`. The reference program is written for one: setup_inputs(seed, part) draws one part's arguments, and reference() takes and returns one part's arrays. A program takes and returns all parts, laid end to end along the dimension named above; each array names one. Nothing has to cross between parts.
All inputs are finite; a program needn't handle non-finite values.
Results may differ from the reference program's by a relative error of at most 0.0056.
Values may be sent and summed in bfloat16 or wider, within the bound.
A program may use at most 64 MiB of HBM per device.

```python
import math
import jax
import jax.numpy as jnp
from jax import lax

R = 512
P_SIZE = 256
CX = 16
ITERS = 2
NX = 64
NY = 64
NZ = 2
N_WIDE = 4


def block_scale(rng, dims, cuts, smallest, top_value):
    factor_of, own = 1.0, jax.random.fold_in(rng, 6)
    for position, shards_of in cuts:
        draws = jnp.exp(jax.random.uniform(jax.random.fold_in(own, position), (shards_of,), jnp.float32, smallest / len(cuts), top_value / len(cuts)))
        factor_of = factor_of * jnp.repeat(draws, dims[position] // shards_of).reshape([-1 if axis == position else 1 for axis in range(len(dims))])
    return factor_of


def noise(rng, extent, deviation, bound, cuts=(), kind=jnp.bfloat16):
    values = jax.random.normal(rng, extent, jnp.float32) * deviation
    if len(cuts) > 0:
        values = block_scale(rng, extent, cuts, -0.22, 0.18) * values
    return jnp.clip(values, min=-bound, max=bound).astype(kind)


def setup_inputs(seed: int = 0, part: int = 0) -> dict:
    keys = jax.random.split(jax.random.key(seed), 6)
    part_splits = jax.random.split(jax.random.fold_in(keys[5], part), 6)
    return {
        "basis": noise(part_splits[0], (NX, NY, NZ, R), R ** -0.5, 0.25, ((0, 4), (1, 4))),
        "kappa": jnp.clip(jnp.exp(math.log(1.0) - 2.3025851 * jax.random.uniform(part_splits[1], (NX, NY, NZ), jnp.float32) ** block_scale(part_splits[1], (NX, NY, NZ), ((0, 4), (1, 4)), -0.2, 0.2)), 0.1, 1.0),
        "velocity": jnp.clip(jax.random.uniform(part_splits[2], (3, P_SIZE), jnp.float32, -2.0, 2.0), -2.0, 2.0),
        "coefficients": noise(part_splits[3], (P_SIZE, R), 1.0, 6.0, (), jnp.float32),
        "propagator": noise(part_splits[4], (R, R), R ** -0.5, 0.25, (), jnp.float32),
    }


step_size = 4.0

def forcing_of(padded, kappa, velocity):
    center = padded[1:-1, 1:-1, 1:-1].astype(jnp.float32)
    x_next = padded[2:, 1:-1, 1:-1].astype(jnp.float32)
    x_prev = padded[:-2, 1:-1, 1:-1].astype(jnp.float32)
    y_next = padded[1:-1, 2:, 1:-1].astype(jnp.float32)
    y_prev = padded[1:-1, :-2, 1:-1].astype(jnp.float32)
    z_next = padded[1:-1, 1:-1, 2:].astype(jnp.float32)
    z_prev = padded[1:-1, 1:-1, :-2].astype(jnp.float32)
    spread = x_next + x_prev + y_next + y_prev + z_next + z_prev - 6.0 * center
    carried = velocity[0] * (x_next * x_next - x_prev * x_prev)
    carried = carried + velocity[1] * (y_next * y_next - y_prev * y_prev)
    carried = carried + velocity[2] * (z_next * z_next - z_prev * z_prev)
    result = kappa[..., None] * spread - 0.25 * carried
    return result.astype(jnp.bfloat16)

def reference(basis, kappa, velocity, coefficients, propagator):
    scale = 1.0 / jnp.sqrt(jnp.float32(NX * NY * NZ))
    state = coefficients
    block_ids = jnp.arange(N_WIDE).astype(jnp.int32)
    for step in range(ITERS):
        lift_rows = state.astype(jnp.bfloat16)

        def lift_block(index):
            rows = lax.dynamic_slice_in_dim(basis, index * CX, CX, 0).reshape(CX * NY * NZ, R)
            made = lax.dot_general(rows, lift_rows, (((1,), (1,)), ((), ())), preferred_element_type=jnp.float32)
            return made.astype(jnp.bfloat16)
        lifted = lax.map(lift_block, block_ids).reshape(NX, NY, NZ, P_SIZE)
        padded = jnp.pad(lifted, ((1, 1), (1, 1), (1, 1), (0, 0)))

        def project_block(total, index):
            window = lax.dynamic_slice_in_dim(padded, index * CX, CX + 2, 0)
            local_kappa = lax.dynamic_slice_in_dim(kappa, index * CX, CX, 0)
            forcing = forcing_of(window, local_kappa, velocity).reshape(CX * NY * NZ, P_SIZE)
            rows = lax.dynamic_slice_in_dim(basis, index * CX, CX, 0).reshape(CX * NY * NZ, R)
            term = lax.dot_general(forcing, rows, (((0,), (0,)), ((), ())), preferred_element_type=jnp.float32)
            return (total + term, None)
        total, unused = lax.scan(project_block, jnp.zeros((P_SIZE, R), jnp.float32), block_ids)
        projected = total * scale
        update = state + step_size * projected
        state = update + jnp.dot(update, propagator.T, precision=lax.Precision.HIGHEST, preferred_element_type=jnp.float32)
    return state
```

```python
import functools
import math

import jax
import jax.numpy as jnp
from jax import lax
from jax.experimental import pallas as pl
from jax.experimental.pallas import tpu as pltpu
from jax.sharding import PartitionSpec as P

ITERS = 2
WIRE = jnp.bfloat16
LANES = 128
CORES = 2

step_size = 4.0

NT = (((1,), (1,)), ((), ()))
NN = (((1,), (0,)), ((), ()))
f32, bf16 = jnp.float32, jnp.bfloat16


def peer(me, offset):
    result, bit = me, 1
    while bit <= offset:
        if offset & bit:
            result = result + (1 - 2 * ((me // bit) % 2)) * bit
        bit *= 2
    return result


def dot(a, b, dims):
    return lax.dot_general(a, b, dims, preferred_element_type=f32)


def kernel(
    chips, narrow, scale,
    basis_hbm, kappa_hbm, velocity_hbm, coefficients_hbm, propagator_hbm, out_ref,
    basis, border, kappa, velocity, coefficients, propagator,
    field, factor, speed, g_high, g_low,
    reduced, landed, kept, mine, gathered,
    load_sem, mate_send, mate_recv, y_send, y_recv, x_send, x_recv,
    r_send, r_recv, g_send, g_recv,
):
    size_x, size_y, size_z, modes = basis_hbm.shape
    slices, depth = basis.shape[:2]
    owned = coefficients.shape[2]
    samples = velocity.shape[1]
    unit = chips * owned
    pitch = size_y * size_z
    half, cells = size_x * pitch, depth * pitch
    tiles = cells // LANES
    x_rows, y_rows = size_y, depth
    y_base = border.shape[1] - 2 * y_rows
    x_base = (y_base - x_rows, 0)
    wide = chips * CORES
    me_w, me_n = lax.axis_index("wide"), lax.axis_index("narrow")
    chip, core = me_w // CORES, me_w % CORES

    def lanes_of(ct):
        return pl.ds(ct * LANES, LANES)

    barrier = pltpu.get_barrier_semaphore()
    greeted = [(e, d) for d in range(narrow) for e in range(wide) if e + d > 0]
    for e, d in greeted:
        pl.semaphore_signal(
            barrier, inc=1, device_id={"wide": peer(me_w, e), "narrow": peer(me_n, d)},
            device_id_type=pl.DeviceIdType.MESH,
        )
    mine_x, theirs_x = pl.ds(core * size_x, size_x), pl.ds((1 - core) * size_x, size_x)
    loads = [
        pltpu.make_async_copy(basis_hbm.at[:, :, :, lanes_of(ct)], basis.at[ct, mine_x], load_sem.at[0])
        for ct in range(slices)
    ]
    for load in loads:
        load.start()
    starts = [
        pltpu.make_async_copy(coefficients_hbm.at[CORES * x + core], coefficients.at[x], load_sem.at[3 + x])
        for x in range(chips)
    ]
    for start in starts:
        start.start()
    own_kappa = pltpu.make_async_copy(kappa_hbm, kappa.at[core], load_sem.at[1])
    own_kappa.start()
    speeds = pltpu.make_async_copy(velocity_hbm, velocity, load_sem.at[2])
    speeds.start()
    inverse = pltpu.make_async_copy(propagator_hbm, propagator, load_sem.at[3 + chips])
    inverse.start()

    def clear(first, count):
        border[:, pl.ds(first, count)] = jnp.zeros((slices, count) + border.shape[2:], bf16)

    pl.when(chip == 0)(lambda: clear(x_base[0], x_rows))
    pl.when(chip == chips - 1)(lambda: clear(x_base[1], x_rows))
    pl.when(me_n == 0)(lambda: clear(y_base, y_rows))
    pl.when(me_n == narrow - 1)(lambda: clear(y_base + y_rows, y_rows))

    pl.semaphore_wait(barrier, len(greeted))

    def remote(src, dst, send, recv, w, n):
        return pltpu.make_async_remote_copy(
            src_ref=src, dst_ref=dst, send_sem=send, recv_sem=recv,
            device_id={"wide": w, "narrow": n}, device_id_type=pl.DeviceIdType.MESH,
        )

    def arrival(ref, send, recv):
        return remote(ref, ref, send, recv, me_w, me_n)

    faces = []
    for j, (from_y, step) in enumerate(((size_y - 1, 1), (0, -1))):
        n = lax.rem(me_n + step + narrow, narrow)
        sends = jnp.logical_and(me_n + step >= 0, me_n + step < narrow)
        receives = jnp.logical_and(me_n - step >= 0, me_n - step < narrow)
        put = pl.ds(y_base + j * y_rows + core * size_x, size_x)
        for k in range(CORES):
            source = core if k == 0 else 1 - core
            came = border.at[:, pl.ds(y_base + j * y_rows + source * size_x, size_x)]
            parts = [
                remote(
                    basis_hbm.at[:, from_y, :, lanes_of(ct)], border.at[ct, put],
                    y_send.at[j, k], y_recv.at[j, k], peer(me_w, k), n,
                )
                for ct in range(slices)
            ]
            faces.append((
                parts, sends, arrival(came, y_send.at[j, k], y_recv.at[j, k]), receives,
            ))
    toward = chip + 2 * core - 1
    x_to = lax.rem(toward + chips, chips)
    sends = jnp.logical_and(toward >= 0, toward < chips)
    put = pl.ds((1 - core) * x_base[1] + core * x_base[0], x_rows)
    if x_base[1] == 0:
        put = pl.ds(core * x_base[0], x_rows)
    for k in range(CORES):
        parts = [
            remote(
                basis_hbm.at[core * (size_x - 1), :, :, lanes_of(ct)], border.at[ct, put],
                x_send.at[k], x_recv.at[core], CORES * x_to + k, me_n,
            )
            for ct in range(slices)
        ]
        came = border.at[:, pl.ds(x_base[1 - k], x_rows)]
        receives = chip < chips - 1 if k == 0 else chip > 0
        faces.append((parts, sends, arrival(came, x_send.at[k], x_recv.at[k]), receives))
    for parts, sends, back, receives in faces:
        def go(parts=parts):
            for part in parts:
                part.start()
        pl.when(sends)(go)
    mate = [
        remote(
            basis_hbm.at[:, :, :, lanes_of(ct)], basis.at[ct, mine_x],
            mate_send.at[0], mate_recv.at[0], peer(me_w, 1), me_n,
        )
        for ct in range(slices)
    ]
    for part in mate:
        part.start()
    mate_back = arrival(basis.at[:, theirs_x], mate_send.at[0], mate_recv.at[0])
    mate_kappa = remote(kappa_hbm, kappa.at[core], mate_send.at[1], mate_recv.at[1], peer(me_w, 1), me_n)
    mate_kappa.start()

    for load in loads:
        load.wait()
    for start in starts:
        start.wait()
    first_rows = jnp.concatenate([
        coefficients[peer(chip, e), peer(me_n, d)].astype(bf16) for d in range(narrow) for e in range(chips)
    ], axis=0)

    def rounded(rows, against):
        return dot(rows, against, NT).astype(bf16).astype(f32)

    def half_of(at):
        return jnp.concatenate([basis[ct, at].reshape(half, LANES) for ct in range(slices)], axis=1)

    def all_cells():
        return jnp.concatenate([basis[ct].reshape(cells, LANES) for ct in range(slices)], axis=1)

    def border_cells():
        return jnp.concatenate(
            [border[ct].reshape(border.shape[1] * size_z, LANES) for ct in range(slices)], axis=1
        )

    outer = pl.ds(cells, border.shape[1] * size_z)
    field[:, pl.ds(pl.multiple_of(core * half, LANES), half)] = rounded(first_rows, half_of(mine_x))

    speeds.wait()
    for k in range(3):
        speed[k] = (0.25 * jnp.broadcast_to(velocity[k:k + 1, :], (LANES, samples))).T

    cell = lax.broadcasted_iota(jnp.int32, (1, cells), 1)
    y_of, z_of = (cell % pitch) // size_z, cell % size_z
    pick = (y_of == lax.broadcasted_iota(jnp.int32, (size_y, cells), 0)).astype(bf16)
    line = lax.broadcasted_iota(jnp.int32, (depth * size_z, cells), 0)
    own_row = (line == (cell // pitch) * size_z + z_of).astype(f32)
    own_kappa.wait()
    mate_kappa.wait_recv()
    rest = kappa[...].reshape(depth * size_z, size_y)
    found = jnp.zeros((depth * size_z, cells), f32)
    for _ in range(3):
        part = rest.astype(bf16)
        rest = rest - part.astype(f32)
        found = found + dot(part, pick, NN)
    factor[...] = jnp.broadcast_to(jnp.sum(found * own_row, axis=0, keepdims=True), factor.shape)

    mate_back.wait_recv()
    field[:, pl.ds(pl.multiple_of((1 - core) * half, LANES), half)] = rounded(first_rows, half_of(theirs_x))
    for parts, sends, back, receives in faces:
        pl.when(receives)(back.wait_recv)
    field[:, outer] = rounded(first_rows, border_cells())

    lane = lax.broadcasted_iota(jnp.int32, (8, LANES), 1)
    lane_x, lane_y, lane_z = lane // pitch, (lane % pitch) // size_z, lane % size_z
    per_tile = LANES // pitch
    low_y, high_y = lane_y == 0, lane_y == size_y - 1
    first_of_tile, last_of_tile = lane < pitch, lane >= LANES - pitch
    from_border = lane_x * size_z + lane_z + jnp.where(high_y, y_rows * size_z, 0)
    z_sign = jnp.where(lane_z == 0, 1.0, -1.0)

    def stencil(first, speeds_of):
        def at(t):
            return field[first:first + 8, t * LANES:(t + 1) * LANES]

        def turn(value, by):
            return pltpu.roll(value, by % LANES, 1)

        v_x, v_y, v_z = speeds_of
        if size_z == 2:
            v_z = v_z * z_sign
        center = [at(t) for t in range(tiles + 1)]
        ahead = [turn(value, -pitch) for value in center]
        behind = [turn(value, pitch) for value in center]
        y_border = at(tiles + 1)
        out = []
        for t in range(tiles):
            mid = center[t]
            x_next = jnp.where(last_of_tile, ahead[t + 1], ahead[t])
            x_prev = jnp.where(first_of_tile, behind[t - 1], behind[t])
            outside = jnp.take_along_axis(y_border, from_border + t * per_tile * size_z, axis=1)
            y_next = jnp.where(high_y, outside, turn(mid, -size_z))
            y_prev = jnp.where(low_y, outside, turn(mid, size_z))
            x_sum, y_sum = x_next + x_prev, y_next + y_prev
            carried = v_x * (x_sum * (x_next - x_prev)) + v_y * (y_sum * (y_next - y_prev))
            if size_z == 2:
                z_sum = jnp.where(lane_z == 0, turn(mid, -1), turn(mid, 1))
                carried = carried + v_z * (z_sum * z_sum)
            else:
                z_next = jnp.where(lane_z < size_z - 1, turn(mid, -1), 0.0)
                z_prev = jnp.where(lane_z > 0, turn(mid, 1), 0.0)
                z_sum = z_next + z_prev
                carried = carried + v_z * (z_sum * (z_next - z_prev))
            spread = x_sum + y_sum + z_sum - 6.0 * mid
            out.append(factor[:, t * LANES:(t + 1) * LANES] * spread - carried)
        return jnp.concatenate(out, axis=1)

    def speeds_at(d, g):
        pieces = [[], [], []]
        for r in range(8 * g, 8 * g + 8, min(8, owned)):
            e, inner = r // owned, r % owned
            row = ((CORES * peer(chip, e) + core) * narrow + peer(me_n, d)) * owned + inner
            count = min(8, owned)
            if count % 8 == 0:
                row = pl.multiple_of(row, 8)
            for k in range(3):
                pieces[k].append(speed[k, pl.ds(row, count), :])
        return [jnp.concatenate(p, axis=0) if len(p) > 1 else p[0] for p in pieces]

    def scatter(d, waits):
        forcing = jnp.concatenate(
            [stencil(d * unit + 8 * g, speeds_at(d, g)) for g in range(unit // 8)], axis=0
        ).astype(bf16)
        total = dot(forcing, all_cells(), NN)
        for e in reversed(range(chips)):
            block = total[e * owned:(e + 1) * owned]
            if d + e == 0:
                kept[...] = block
                continue
            copy = remote(
                reduced.at[d, e], landed.at[d, e], r_send.at[d, e], r_recv.at[d, e],
                CORES * peer(chip, e) + core, peer(me_n, d),
            )
            if waits:
                copy.wait_send()
            reduced[d, e] = block.astype(WIRE)
            copy.start()

    def all_sends(ref, sends, recvs):
        for d in range(narrow):
            for e in range(chips):
                if d + e > 0:
                    arrival(ref(d, e), sends.at[d, e], recvs.at[d, e]).wait_send()

    state = coefficients[chip, me_n]
    for step in range(ITERS):
        for d in range(narrow) if step else reversed(range(narrow)):
            if step > 0:
                blocks = []
                for e in range(chips):
                    if d + e == 0:
                        blocks.append(mine[...])
                    else:
                        arrival(gathered.at[d, e], g_send.at[d, e], g_recv.at[d, e]).wait_recv()
                        blocks.append(gathered[d, e])
                rows = jnp.concatenate(blocks, axis=0)
                field[d * unit:(d + 1) * unit, :cells] = rounded(rows, all_cells())
                field[d * unit:(d + 1) * unit, outer] = rounded(rows, border_cells())
            scatter(d, step > 0)

        if step == 0:
            inverse.wait()
            high = propagator[...].astype(bf16)
            g_high[...] = high.T
            g_low[...] = (propagator[...] - high.astype(f32)).astype(bf16).T

        summed = kept[...]
        for d in range(narrow):
            for e in range(chips):
                if d + e > 0:
                    arrival(landed.at[d, e], r_send.at[d, e], r_recv.at[d, e]).wait_recv()
                    summed = summed + landed[d, e].astype(f32)

        update = state + step_size * (summed * scale)
        high = update.astype(bf16)
        low = (update - high.astype(f32)).astype(bf16)
        both = dot(jnp.concatenate([high, low], axis=0), g_high[...], NN)
        small = both[owned:] + dot(high, g_low[...], NN)
        state = update + (both[:owned] + small)

        if step + 1 < ITERS:
            if step > 0:
                all_sends(lambda d, e: mine, g_send, g_recv)
            mine[...] = state.astype(bf16)
            for d in reversed(range(narrow)):
                for e in reversed(range(chips)):
                    if d + e > 0:
                        remote(
                            mine, gathered.at[d, e], g_send.at[d, e], g_recv.at[d, e],
                            CORES * peer(chip, e) + core, peer(me_n, d),
                        ).start()

    out_ref[...] = state
    all_sends(lambda d, e: reduced.at[d, e], r_send, r_recv)
    all_sends(lambda d, e: mine, g_send, g_recv)
    for parts, sends, back, receives in faces:
        def sent(parts=parts):
            for part in parts:
                part.wait_send()
        pl.when(sends)(sent)
    for part in mate:
        part.wait_send()
    mate_kappa.wait_send()


def body(basis, kappa, velocity, coefficients, propagator):
    size_x, size_y, size_z, modes = basis.shape
    samples = coefficients.shape[0]
    wide, narrow = lax.axis_size("wide"), lax.axis_size("narrow")
    chips = wide // CORES
    owned = samples // (wide * narrow)
    unit = chips * owned
    scale = 1.0 / math.sqrt(size_x * size_y * size_z * wide * narrow)
    pitch = size_y * size_z
    depth = CORES * size_x
    cells = depth * pitch
    assert LANES % pitch == 0 and cells % LANES == 0 and 2 * pitch <= LANES
    assert 2 * depth * size_z == LANES and unit % 8 == 0
    border = 2 * LANES // size_z
    dma = pltpu.SemaphoreType.DMA
    hbm = pl.BlockSpec(memory_space=pltpu.HBM)
    inputs = (
        basis, kappa.transpose(0, 2, 1), velocity,
        coefficients.reshape(wide, narrow, owned, modes), propagator,
    )
    return pl.pallas_call(
        functools.partial(kernel, chips, narrow, scale),
        out_shape=jax.ShapeDtypeStruct((owned, modes), f32),
        in_specs=[hbm] * len(inputs),
        out_specs=pl.BlockSpec(memory_space=pltpu.VMEM),
        scratch_shapes=[
            pltpu.VMEM((modes // LANES, depth, size_y, size_z, LANES), bf16),
            pltpu.VMEM((modes // LANES, border, size_z, LANES), bf16),
            pltpu.VMEM((CORES, size_x, size_z, size_y), f32),
            pltpu.VMEM((3, samples), f32),
            pltpu.VMEM((chips, narrow, owned, modes), f32),
            pltpu.VMEM((modes, modes), f32),
            pltpu.VMEM((narrow * unit, cells + border * size_z), f32),
            pltpu.VMEM((8, cells), f32),
            pltpu.VMEM((3, samples, LANES), f32),
            pltpu.VMEM((modes, modes), bf16),
            pltpu.VMEM((modes, modes), bf16),
            pltpu.VMEM((narrow, chips, owned, modes), WIRE),
            pltpu.VMEM((narrow, chips, owned, modes), WIRE),
            pltpu.VMEM((owned, modes), f32),
            pltpu.VMEM((owned, modes), bf16),
            pltpu.VMEM((narrow, chips, owned, modes), bf16),
            dma((4 + chips,)), dma((2,)), dma((2,)),
            dma((2, CORES)), dma((2, CORES)), dma((CORES,)), dma((CORES,)),
            dma((narrow, chips)), dma((narrow, chips)),
            dma((narrow, chips)), dma((narrow, chips)),
        ],
        compiler_params=pltpu.CompilerParams(
            collective_id=0, has_side_effects=True, vmem_limit_bytes=48 * 1024 * 1024
        ),
    )(*(pltpu.with_memory_space_constraint(value, pltpu.HBM) for value in inputs))


def solution(mesh):
    placed = (
        P(("groups", "wide"), "narrow", None, None),
        P(("groups", "wide"), "narrow", None),
        P(None, "groups"),
        P("groups", None),
        P("groups", None),
    )
    return jax.shard_map(
        body,
        mesh=mesh,
        in_specs=placed,
        out_specs=P(("groups", "wide", "narrow"), None),
        check_vma=False,
    )
```

```python
import functools
import math

import jax
import jax.numpy as jnp
from jax import lax
from jax.experimental import pallas as pl
from jax.experimental.pallas import tpu as pltpu
from jax.sharding import PartitionSpec as P

ITERS = 2
WIRE = jnp.bfloat16
LANES = 128
CORES = 2

step_size = 4.0

NT = (((1,), (1,)), ((), ()))
NN = (((1,), (0,)), ((), ()))
f32, bf16 = jnp.float32, jnp.bfloat16


def peer(me, offset):
    result, bit = me, 1
    while bit <= offset:
        if offset & bit:
            result = result + (1 - 2 * ((me // bit) % 2)) * bit
        bit *= 2
    return result


def dot(a, b, dims):
    return lax.dot_general(a, b, dims, preferred_element_type=f32)


def kernel(
    chips, narrow, scale,
    basis_hbm, kappa_hbm, velocity_hbm, coefficients_hbm, propagator_hbm, out_ref,
    basis, border, kappa, velocity, coefficients, propagator,
    rows_of, columns_of, field, factor, speed, g_high, g_low,
    reduced, landed, kept, mine, gathered,
    load_sem, mate_recv, face_recv, out_send,
    r_send, r_recv, g_send, g_recv, word,
):
    size_x, size_y, size_z, modes = basis_hbm.shape
    slices, depth = basis.shape[:2]
    owned = coefficients.shape[2]
    samples = velocity.shape[1]
    unit = chips * owned
    pitch = size_y * size_z
    half, cells = size_x * pitch, depth * pitch
    tiles = cells // LANES
    x_rows, y_rows = size_y, depth
    y_base = border.shape[1] - 2 * y_rows
    x_base = (y_base - x_rows, 0)
    wide = chips * CORES
    me_w, me_n = lax.axis_index("wide"), lax.axis_index("narrow")
    chip, core = me_w // CORES, me_w % CORES

    def lanes_of(ct):
        return pl.ds(ct * LANES, LANES)

    barrier = pltpu.get_barrier_semaphore()

    def greet(w, n):
        pl.semaphore_signal(
            barrier, inc=1, device_id={"wide": w, "narrow": n}, device_id_type=pl.DeviceIdType.MESH
        )

    greet(peer(me_w, 1), me_n)
    greetings = 1
    for step in (-1, 1):
        n, x = me_n + step, chip + step
        n_there = jnp.logical_and(n >= 0, n < narrow)
        x_there = jnp.logical_and(x >= 0, x < chips)

        def along_narrow(n=n):
            for k in range(CORES):
                greet(peer(me_w, k), n)

        def along_wide(x=x):
            for k in range(CORES):
                greet(CORES * x + k, me_n)

        pl.when(n_there)(along_narrow)
        pl.when(x_there)(along_wide)
        greetings = greetings + CORES * (jnp.where(n_there, 1, 0) + jnp.where(x_there, 1, 0))
    mine_x, theirs_x = pl.ds(core * size_x, size_x), pl.ds((1 - core) * size_x, size_x)
    loads = [
        pltpu.make_async_copy(basis_hbm.at[:, :, :, lanes_of(ct)], basis.at[ct, mine_x], load_sem.at[0])
        for ct in range(slices)
    ]
    loaded = pltpu.make_async_copy(basis.at[:, mine_x], basis.at[:, mine_x], load_sem.at[0])
    for load in loads:
        load.start()
    starts = [
        pltpu.make_async_copy(coefficients_hbm.at[CORES * x + core], coefficients.at[x], load_sem.at[3])
        for x in range(chips)
    ]
    started = pltpu.make_async_copy(coefficients, coefficients, load_sem.at[3])
    for start in starts:
        start.start()
    own_kappa = pltpu.make_async_copy(kappa_hbm, kappa.at[core], load_sem.at[1])
    own_kappa.start()
    speeds = pltpu.make_async_copy(velocity_hbm, velocity, load_sem.at[4])
    speeds.start()
    inverse = pltpu.make_async_copy(propagator_hbm, propagator, load_sem.at[2])
    inverse.start()

    def clear(first, count):
        border[:, pl.ds(first, count)] = jnp.zeros((slices, count) + border.shape[2:], bf16)

    pl.when(chip == 0)(lambda: clear(x_base[0], x_rows))
    pl.when(chip == chips - 1)(lambda: clear(x_base[1], x_rows))
    pl.when(me_n == 0)(lambda: clear(y_base, y_rows))
    pl.when(me_n == narrow - 1)(lambda: clear(y_base + y_rows, y_rows))

    pl.semaphore_wait(barrier, greetings)

    def lines(count, at, where, forth, back):
        def tell(sem, step):
            pl.semaphore_signal(
                sem, inc=1, device_id=where(at + step), device_id_type=pl.DeviceIdType.MESH
            )

        def begin():
            pl.when(at == 0)(lambda: tell(forth, 1))
            pl.when(at == count - 1)(lambda: tell(back, -1))

        def go_on():
            @pl.when(jnp.logical_and(at > 0, at < count - 1))
            def _():
                pl.semaphore_wait(forth, 1)
                tell(forth, 1)
                pl.semaphore_wait(back, 1)
                tell(back, -1)

        def end():
            pl.when(at == count - 1)(lambda: pl.semaphore_wait(forth, 1))
            pl.when(at == 0)(lambda: pl.semaphore_wait(back, 1))

        return begin, go_on, end

    if chips > 2:
        for phase in lines(
            chips, chip, lambda x: {"wide": CORES * x + core, "narrow": me_n}, word.at[2], word.at[3]
        ):
            phase()
    all_in_begin, all_in_go_on, all_in = lines(
        narrow, me_n, lambda n: {"wide": me_w, "narrow": n}, word.at[0], word.at[1]
    )
    all_in_begin()

    def remote(src, dst, send, recv, w, n):
        return pltpu.make_async_remote_copy(
            src_ref=src, dst_ref=dst, send_sem=send, recv_sem=recv,
            device_id={"wide": w, "narrow": n}, device_id_type=pl.DeviceIdType.MESH,
        )

    def arrival(ref, send, recv):
        return remote(ref, ref, send, recv, me_w, me_n)

    faces = []
    for j, (from_y, step) in enumerate(((size_y - 1, 1), (0, -1))):
        n = lax.rem(me_n + step + narrow, narrow)
        first = y_base + j * y_rows
        parts = [
            remote(
                basis_hbm.at[:, from_y, :, lanes_of(ct)], border.at[ct, pl.ds(first + core * size_x, size_x)],
                out_send.at[j], face_recv.at[j], peer(me_w, k), n,
            )
            for k in range(CORES) for ct in range(slices)
        ]
        came = arrival(border.at[:, pl.ds(first, y_rows)], out_send.at[j], face_recv.at[j])
        faces.append((
            parts, jnp.logical_and(me_n + step >= 0, me_n + step < narrow), came,
            [(came, jnp.logical_and(me_n - step >= 0, me_n - step < narrow))],
        ))
    toward = chip + 2 * core - 1
    x_to = lax.rem(toward + chips, chips)
    parts = [
        remote(
            basis_hbm.at[core * (size_x - 1), :, :, lanes_of(ct)], border.at[ct, pl.ds(core * x_base[0], x_rows)],
            out_send.at[2], face_recv.at[2 + core], CORES * x_to + k, me_n,
        )
        for k in range(CORES) for ct in range(slices)
    ]
    faces.append((
        parts, jnp.logical_and(toward >= 0, toward < chips),
        arrival(border.at[:, pl.ds(0, CORES * x_rows)], out_send.at[2], face_recv.at[2]),
        [
            (arrival(border.at[:, pl.ds(k * x_base[0], x_rows)], out_send.at[2], face_recv.at[2 + k]), there)
            for k, there in ((0, chip < chips - 1), (1, chip > 0))
        ],
    ))
    for parts, sends, gone, comes in faces:
        def go(parts=parts):
            for part in parts:
                part.start()
        pl.when(sends)(go)
    mate = [
        remote(
            basis_hbm.at[:, :, :, lanes_of(ct)], basis.at[ct, mine_x],
            out_send.at[3], mate_recv.at[0], peer(me_w, 1), me_n,
        )
        for ct in range(slices)
    ]
    for part in mate:
        part.start()
    mate_gone = arrival(basis.at[:, mine_x], out_send.at[3], mate_recv.at[0])
    mate_back = arrival(basis.at[:, theirs_x], out_send.at[3], mate_recv.at[0])
    mate_kappa = remote(kappa_hbm, kappa.at[core], out_send.at[4], mate_recv.at[1], peer(me_w, 1), me_n)
    mate_kappa.start()

    loaded.wait()
    started.wait()

    def arrange(first, blocks, keep):
        values = jnp.concatenate([block.reshape(-1, LANES) for block in blocks], axis=1)
        count = values.shape[0]
        if keep:
            rows_of[pl.ds(first, count), :] = values
        columns_of[:, pl.ds(first, count)] = values.T

    arrange(pl.multiple_of(core * half, half), [basis[ct, mine_x] for ct in range(slices)], True)

    speeds.wait()
    own_kappa.wait()
    for k in range(3):
        speed[k] = (0.25 * jnp.broadcast_to(velocity[k:k + 1, :], (LANES, samples))).T

    all_in_go_on()
    mate_back.wait_recv()
    mate_kappa.wait_recv()
    arrange(pl.multiple_of((1 - core) * half, half), [basis[ct, theirs_x] for ct in range(slices)], True)

    def rounded(rows, at):
        return dot(rows, columns_of[:, at], NN).astype(bf16).astype(f32)

    first_rows = jnp.concatenate([
        coefficients[peer(chip, e), peer(me_n, d)].astype(bf16) for d in range(narrow) for e in range(chips)
    ], axis=0)
    inner, outer = slice(0, cells), slice(cells, cells + border.shape[1] * size_z)
    field[:, inner] = rounded(first_rows, inner)

    cell = lax.broadcasted_iota(jnp.int32, (1, cells), 1)
    y_of, z_of = (cell % pitch) // size_z, cell % size_z
    pick = (y_of == lax.broadcasted_iota(jnp.int32, (size_y, cells), 0)).astype(bf16)
    line = lax.broadcasted_iota(jnp.int32, (depth * size_z, cells), 0)
    own_row = (line == (cell // pitch) * size_z + z_of).astype(f32)
    rest = kappa[...].reshape(depth * size_z, size_y)
    found = jnp.zeros((depth * size_z, cells), f32)
    for _ in range(3):
        part = rest.astype(bf16)
        rest = rest - part.astype(f32)
        found = found + dot(part, pick, NN)
    factor[...] = jnp.broadcast_to(jnp.sum(found * own_row, axis=0, keepdims=True), factor.shape)

    for parts, sends, gone, comes in faces:
        for came, there in comes:
            pl.when(there)(came.wait_recv)
    arrange(cells, [border[ct] for ct in range(slices)], False)
    field[:, outer] = rounded(first_rows, outer)

    lane = lax.broadcasted_iota(jnp.int32, (8, LANES), 1)
    lane_x, lane_y, lane_z = lane // pitch, (lane % pitch) // size_z, lane % size_z
    per_tile = LANES // pitch
    low_y, high_y = lane_y == 0, lane_y == size_y - 1
    first_of_tile, last_of_tile = lane < pitch, lane >= LANES - pitch
    from_border = lane_x * size_z + lane_z + jnp.where(high_y, y_rows * size_z, 0)
    z_sign = jnp.where(lane_z == 0, 1.0, -1.0)

    def stencil(first, speeds_of):
        def at(t):
            return field[first:first + 8, t * LANES:(t + 1) * LANES]

        def turn(value, by):
            return pltpu.roll(value, by % LANES, 1)

        v_x, v_y, v_z = speeds_of
        if size_z == 2:
            v_z = v_z * z_sign
        center = [at(t) for t in range(tiles + 1)]
        ahead = [turn(value, -pitch) for value in center]
        behind = [turn(value, pitch) for value in center]
        y_border = at(tiles + 1)
        out = []
        for t in range(tiles):
            mid = center[t]
            x_next = jnp.where(last_of_tile, ahead[t + 1], ahead[t])
            x_prev = jnp.where(first_of_tile, behind[t - 1], behind[t])
            outside = jnp.take_along_axis(y_border, from_border + t * per_tile * size_z, axis=1)
            y_next = jnp.where(high_y, outside, turn(mid, -size_z))
            y_prev = jnp.where(low_y, outside, turn(mid, size_z))
            x_sum, y_sum = x_next + x_prev, y_next + y_prev
            carried = v_x * (x_sum * (x_next - x_prev)) + v_y * (y_sum * (y_next - y_prev))
            if size_z == 2:
                z_sum = jnp.where(lane_z == 0, turn(mid, -1), turn(mid, 1))
                carried = carried + v_z * (z_sum * z_sum)
            else:
                z_next = jnp.where(lane_z < size_z - 1, turn(mid, -1), 0.0)
                z_prev = jnp.where(lane_z > 0, turn(mid, 1), 0.0)
                z_sum = z_next + z_prev
                carried = carried + v_z * (z_sum * (z_next - z_prev))
            spread = x_sum + y_sum + z_sum - 6.0 * mid
            out.append(factor[:, t * LANES:(t + 1) * LANES] * spread - carried)
        return jnp.concatenate(out, axis=1)

    def speeds_at(d, g):
        pieces = [[], [], []]
        for r in range(8 * g, 8 * g + 8, min(8, owned)):
            e, inner = r // owned, r % owned
            row = ((CORES * peer(chip, e) + core) * narrow + peer(me_n, d)) * owned + inner
            count = min(8, owned)
            if count % 8 == 0:
                row = pl.multiple_of(row, 8)
            for k in range(3):
                pieces[k].append(speed[k, pl.ds(row, count), :])
        return [jnp.concatenate(p, axis=0) if len(p) > 1 else p[0] for p in pieces]

    def slot(d, e):
        return d * chips + e - 1

    def scatter(group):
        forcing = jnp.concatenate(
            [stencil(d * unit + 8 * g, speeds_at(d, g)) for d in group for g in range(unit // 8)], axis=0
        ).astype(bf16)
        total = dot(forcing, rows_of[...], NN)
        copies = []
        for i, d in enumerate(group):
            for e in reversed(range(chips)):
                block = total[i * unit + e * owned:i * unit + (e + 1) * owned]
                if d + e == 0:
                    kept[...] = block
                    continue
                reduced[slot(d, e)] = block.astype(WIRE)
                copies.append(remote(
                    reduced.at[slot(d, e)], landed.at[slot(d, e)], r_send, r_recv,
                    CORES * peer(chip, e) + core, peer(me_n, d),
                ))
        return copies

    def each(there):
        for d in range(narrow):
            for e in range(chips):
                if d + e > 0:
                    there(d, e)

    def reduced_sent():
        arrival(reduced, r_send, r_recv).wait_send()

    def mine_sent():
        arrival(reduced, g_send, r_recv).wait_send()

    near_first = [tuple(range(narrow // 2))] + [(d,) for d in range(narrow // 2, narrow)]
    far_first = [tuple(range(narrow // 2, narrow))[::-1], tuple(range(narrow // 2))[::-1]]
    state = coefficients[chip, me_n]
    for step in range(ITERS):
        if step > 0:
            reduced_sent()
        for number, group in enumerate(near_first if step else far_first):
            if step > 0:
                blocks = []
                for d in group:
                    beyond = gathered.at[d] if d > 0 else gathered.at[0, pl.ds(1, chips - 1)]
                    arrival(beyond, g_send, g_recv.at[d]).wait_recv()
                for d in group:
                    for e in range(chips):
                        blocks.append(gathered[d, e] if d + e > 0 else mine[...])
                rows = jnp.concatenate(blocks, axis=0)
                at = slice(group[0] * unit, (group[-1] + 1) * unit)
                field[at, :] = rounded(rows, slice(None))
            copies = scatter(group)
            if step == 0 and number == 0:
                all_in()
            for copy in copies:
                copy.start()

        if step == 0:
            inverse.wait()
            high = propagator[...].astype(bf16)
            g_high[...] = high.T
            g_low[...] = (propagator[...] - high.astype(f32)).astype(bf16).T

        arrival(landed, r_send, r_recv).wait_recv()
        parts = [kept[...]]
        each(lambda d, e: parts.append(landed[slot(d, e)].astype(f32)))
        summed = sum(parts[1:], parts[0])

        update = state + step_size * (summed * scale)
        high = update.astype(bf16)
        low = (update - high.astype(f32)).astype(bf16)
        both = dot(jnp.concatenate([high, low], axis=0), g_high[...], NN)
        small = both[owned:] + dot(high, g_low[...], NN)
        state = update + (both[:owned] + small)

        if step + 1 < ITERS:
            if step > 0:
                mine_sent()
            mine[...] = state.astype(bf16)
            for d in reversed(range(narrow)):
                for e in reversed(range(chips)):
                    if d + e > 0:
                        remote(
                            mine, gathered.at[d, e], g_send, g_recv.at[d],
                            CORES * peer(chip, e) + core, peer(me_n, d),
                        ).start()

    out_ref[...] = state
    reduced_sent()
    mine_sent()
    for parts, sends, gone, comes in faces:
        pl.when(sends)(gone.wait_send)
    mate_gone.wait_send()
    mate_kappa.wait_send()


def body(basis, kappa, velocity, coefficients, propagator):
    size_x, size_y, size_z, modes = basis.shape
    samples = coefficients.shape[0]
    wide, narrow = lax.axis_size("wide"), lax.axis_size("narrow")
    chips = wide // CORES
    owned = samples // (wide * narrow)
    unit = chips * owned
    scale = 1.0 / math.sqrt(size_x * size_y * size_z * wide * narrow)
    pitch = size_y * size_z
    depth = CORES * size_x
    cells = depth * pitch
    assert LANES % pitch == 0 and cells % LANES == 0 and 2 * pitch <= LANES
    assert 2 * depth * size_z == LANES and unit % 8 == 0
    border = 2 * LANES // size_z
    dma = pltpu.SemaphoreType.DMA
    hbm = pl.BlockSpec(memory_space=pltpu.HBM)
    inputs = (
        basis, kappa.transpose(0, 2, 1), velocity,
        coefficients.reshape(wide, narrow, owned, modes), propagator,
    )
    return pl.pallas_call(
        functools.partial(kernel, chips, narrow, scale),
        out_shape=jax.ShapeDtypeStruct((owned, modes), f32),
        in_specs=[hbm] * len(inputs),
        out_specs=pl.BlockSpec(memory_space=pltpu.VMEM),
        scratch_shapes=[
            pltpu.VMEM((modes // LANES, depth, size_y, size_z, LANES), bf16),
            pltpu.VMEM((modes // LANES, border, size_z, LANES), bf16),
            pltpu.VMEM((CORES, size_x, size_z, size_y), f32),
            pltpu.VMEM((3, samples), f32),
            pltpu.VMEM((chips, narrow, owned, modes), f32),
            pltpu.VMEM((modes, modes), f32),
            pltpu.VMEM((cells, modes), bf16),
            pltpu.VMEM((modes, cells + border * size_z), bf16),
            pltpu.VMEM((narrow * unit, cells + border * size_z), f32),
            pltpu.VMEM((8, cells), f32),
            pltpu.VMEM((3, samples, LANES), f32),
            pltpu.VMEM((modes, modes), bf16),
            pltpu.VMEM((modes, modes), bf16),
            pltpu.VMEM((narrow * chips - 1, owned, modes), WIRE),
            pltpu.VMEM((narrow * chips - 1, owned, modes), WIRE),
            pltpu.VMEM((owned, modes), f32),
            pltpu.VMEM((owned, modes), bf16),
            pltpu.VMEM((narrow, chips, owned, modes), bf16),
            dma((5,)), dma((2,)), dma((4,)), dma((5,)), dma, dma, dma, dma((narrow,)),
            pltpu.SemaphoreType.REGULAR((4 if chips > 2 else 2,)),
        ],
        compiler_params=pltpu.CompilerParams(
            collective_id=0, has_side_effects=True, vmem_limit_bytes=48 * 1024 * 1024
        ),
    )(*(pltpu.with_memory_space_constraint(value, pltpu.HBM) for value in inputs))


def solution(mesh):
    placed = (
        P(("groups", "wide"), "narrow", None, None),
        P(("groups", "wide"), "narrow", None),
        P(None, "groups"),
        P("groups", None),
        P("groups", None),
    )
    return jax.shard_map(
        body,
        mesh=mesh,
        in_specs=placed,
        out_specs=P(("groups", "wide", "narrow"), None),
        check_vma=False,
    )
```

```python
import functools
import math

import jax
import jax.numpy as jnp
from jax import lax
from jax.experimental import pallas as pl
from jax.experimental.pallas import tpu as pltpu
from jax.sharding import PartitionSpec as P

ITERS = 2
WIRE = jnp.bfloat16
LANES = 128
CORES = 2

step_size = 4.0

NT = (((1,), (1,)), ((), ()))
NN = (((1,), (0,)), ((), ()))
f32, bf16 = jnp.float32, jnp.bfloat16


def peer(me, offset):
    result, bit = me, 1
    while bit <= offset:
        if offset & bit:
            result = result + (1 - 2 * ((me // bit) % 2)) * bit
        bit *= 2
    return result


def dot(a, b, dims):
    return lax.dot_general(a, b, dims, preferred_element_type=f32)


def kernel(
    chips, narrow, scale,
    basis_hbm, kappa_hbm, velocity_hbm, coefficients_hbm, propagator_hbm, out_ref,
    basis, border, kappa, velocity, coefficients, propagator,
    edge_out, edge_in, edge_of, rows_of, columns_of, field, factor, speed, g_high, g_low,
    reduced, landed, kept, mine, gathered,
    load_sem, mate_recv, face_recv, out_send,
    r_send, r_recv, g_send, g_recv, edge_send, edge_recv, word,
):
    size_x, size_y, size_z, modes = basis_hbm.shape
    slices, depth = basis.shape[:2]
    owned = coefficients.shape[2]
    samples = velocity.shape[1]
    unit = chips * owned
    pitch = size_y * size_z
    half, cells = size_x * pitch, depth * pitch
    tiles = cells // LANES
    x_rows, y_rows = size_y, depth
    y_base = border.shape[1] - 2 * y_rows
    x_base = (y_base - x_rows, 0)
    wide = chips * CORES
    me_w, me_n = lax.axis_index("wide"), lax.axis_index("narrow")
    chip, core = me_w // CORES, me_w % CORES
    far_x, far_n = chips // 2, narrow // 2

    def lanes_of(ct):
        return pl.ds(ct * LANES, LANES)

    barrier = pltpu.get_barrier_semaphore()

    def greet(w, n):
        pl.semaphore_signal(
            barrier, inc=1, device_id={"wide": w, "narrow": n}, device_id_type=pl.DeviceIdType.MESH
        )

    greet(peer(me_w, 1), me_n)
    greetings = 1
    for step in (-1, 1):
        n, x = me_n + step, chip + step
        n_there = jnp.logical_and(n >= 0, n < narrow)
        x_there = jnp.logical_and(x >= 0, x < chips)

        def along_narrow(n=n):
            for k in range(CORES):
                greet(peer(me_w, k), n)

        def along_wide(x=x):
            for k in range(CORES):
                greet(CORES * x + k, me_n)

        pl.when(n_there)(along_narrow)
        pl.when(x_there)(along_wide)
        greetings = greetings + CORES * (jnp.where(n_there, 1, 0) + jnp.where(x_there, 1, 0))
    mine_x, theirs_x = pl.ds(core * size_x, size_x), pl.ds((1 - core) * size_x, size_x)
    loads = [
        pltpu.make_async_copy(basis_hbm.at[:, :, :, lanes_of(ct)], basis.at[ct, mine_x], load_sem.at[0])
        for ct in range(slices)
    ]
    loaded = pltpu.make_async_copy(basis.at[:, mine_x], basis.at[:, mine_x], load_sem.at[0])
    for load in loads:
        load.start()
    started = pltpu.make_async_copy(coefficients_hbm, coefficients, load_sem.at[3])
    started.start()
    own_kappa = pltpu.make_async_copy(kappa_hbm, kappa.at[core], load_sem.at[1])
    own_kappa.start()
    speeds = pltpu.make_async_copy(velocity_hbm, velocity, load_sem.at[4])
    speeds.start()
    inverse = pltpu.make_async_copy(propagator_hbm, propagator, load_sem.at[2])

    def clear(first, count):
        border[:, pl.ds(first, count)] = jnp.zeros((slices, count) + border.shape[2:], bf16)
        at = slice(first * size_z, (first + count) * size_z)
        edge_in[at, :] = jnp.zeros((count * size_z, edge_in.shape[1]), bf16)

    pl.when(chip == 0)(lambda: clear(x_base[0], x_rows))
    pl.when(chip == chips - 1)(lambda: clear(x_base[1], x_rows))
    pl.when(me_n == 0)(lambda: clear(y_base, y_rows))
    pl.when(me_n == narrow - 1)(lambda: clear(y_base + y_rows, y_rows))

    pl.semaphore_wait(barrier, greetings)

    def lines(count, at, where, forth, back):
        def tell(sem, step):
            pl.semaphore_signal(
                sem, inc=1, device_id=where(at + step), device_id_type=pl.DeviceIdType.MESH
            )

        def begin():
            pl.when(at == 0)(lambda: tell(forth, 1))
            pl.when(at == count - 1)(lambda: tell(back, -1))

        def go_on():
            @pl.when(jnp.logical_and(at > 0, at < count - 1))
            def _():
                pl.semaphore_wait(forth, 1)
                tell(forth, 1)
                pl.semaphore_wait(back, 1)
                tell(back, -1)

        def end():
            pl.when(at == count - 1)(lambda: pl.semaphore_wait(forth, 1))
            pl.when(at == 0)(lambda: pl.semaphore_wait(back, 1))

        return begin, go_on, end

    if chips > 2:
        for phase in lines(
            chips, chip, lambda x: {"wide": CORES * x + core, "narrow": me_n}, word.at[2], word.at[3]
        ):
            phase()
    all_in_begin, all_in_go_on, all_in = lines(
        narrow, me_n, lambda n: {"wide": me_w, "narrow": n}, word.at[0], word.at[1]
    )
    all_in_begin()

    def remote(src, dst, send, recv, w, n):
        return pltpu.make_async_remote_copy(
            src_ref=src, dst_ref=dst, send_sem=send, recv_sem=recv,
            device_id={"wide": w, "narrow": n}, device_id_type=pl.DeviceIdType.MESH,
        )

    def arrival(ref, send, recv):
        return remote(ref, ref, send, recv, me_w, me_n)

    faces, edges = [], []
    line_x, line_y = size_y * size_z, size_x * size_z

    def edge(face, first, count, number, came, w, n):
        parts = [
            remote(
                edge_out.at[k, pl.ds(face[0], face[1])], edge_in.at[pl.ds(first, count)],
                edge_send.at[number], edge_recv.at[came], w(k), n,
            )
            for k in range(CORES)
        ]
        gone = arrival(edge_in.at[pl.ds(0, CORES * count)], edge_send.at[number], edge_recv.at[came])
        return parts, gone

    def whole_edge(first, count, number):
        return arrival(edge_in.at[pl.ds(first * size_z, count * size_z)], edge_send.at[0], edge_recv.at[number])

    for j, (from_y, step) in enumerate(((size_y - 1, 1), (0, -1))):
        n = lax.rem(me_n + step + narrow, narrow)
        first = y_base + j * y_rows
        parts = [
            remote(
                basis_hbm.at[:, from_y, :, lanes_of(ct)], border.at[ct, pl.ds(first + core * size_x, size_x)],
                out_send.at[j], face_recv.at[j], peer(me_w, k), n,
            )
            for k in range(CORES) for ct in range(slices)
        ]
        came = arrival(border.at[:, pl.ds(first, y_rows)], out_send.at[j], face_recv.at[j])
        goes = jnp.logical_and(me_n + step >= 0, me_n + step < narrow)
        there = jnp.logical_and(me_n - step >= 0, me_n - step < narrow)
        faces.append((parts, goes, came, [(came, there)]))
        at = pl.multiple_of(first * size_z + core * line_y, line_y)
        parts, gone = edge((j * line_y, line_y), at, line_y, j, j, lambda k: CORES * chip + k, n)
        edges.append((parts, goes, gone, [(whole_edge(first, y_rows, j), there)]))
    toward = chip + 2 * core - 1
    x_to = lax.rem(toward + chips, chips)
    parts = [
        remote(
            basis_hbm.at[core * (size_x - 1), :, :, lanes_of(ct)], border.at[ct, pl.ds(core * x_base[0], x_rows)],
            out_send.at[2], face_recv.at[2 + core], CORES * x_to + k, me_n,
        )
        for k in range(CORES) for ct in range(slices)
    ]
    goes = jnp.logical_and(toward >= 0, toward < chips)
    faces.append((
        parts, goes,
        arrival(border.at[:, pl.ds(0, CORES * x_rows)], out_send.at[2], face_recv.at[2]),
        [
            (arrival(border.at[:, pl.ds(k * x_base[0], x_rows)], out_send.at[2], face_recv.at[2 + k]), there)
            for k, there in ((0, chip < chips - 1), (1, chip > 0))
        ],
    ))
    at = pl.multiple_of(core * (x_base[0] * size_z), line_x)
    parts, gone = edge((2 * line_y, line_x), at, line_x, 2, 2 + core, lambda k: CORES * x_to + k, me_n)
    edges.append((parts, goes, gone, [
        (whole_edge(k * x_base[0], x_rows, 2 + k), there) for k, there in ((0, chip < chips - 1), (1, chip > 0))
    ]))

    def send_all(copies):
        for parts, sends, gone, comes in copies:
            def go(parts=parts):
                for part in parts:
                    part.start()
            pl.when(sends)(go)

    def take_all(copies):
        for parts, sends, gone, comes in copies:
            for came, there in comes:
                pl.when(there)(came.wait_recv)

    mate = [
        remote(
            basis_hbm.at[:, :, :, lanes_of(ct)], basis.at[ct, mine_x],
            out_send.at[3], mate_recv.at[0], peer(me_w, 1), me_n,
        )
        for ct in range(slices)
    ]
    for part in mate:
        part.start()
    mate_gone = arrival(basis.at[:, mine_x], out_send.at[3], mate_recv.at[0])
    mate_back = arrival(basis.at[:, theirs_x], out_send.at[3], mate_recv.at[0])
    mate_kappa = remote(kappa_hbm, kappa.at[core], out_send.at[4], mate_recv.at[1], peer(me_w, 1), me_n)
    mate_kappa.start()

    loaded.wait()
    started.wait()
    inverse.start()

    def in_tiles(of):
        return jnp.concatenate([of(ct).reshape(-1, LANES) for ct in range(slices)], axis=1)

    own_edge = jnp.concatenate([
        in_tiles(lambda ct: basis[ct, mine_x, size_y - 1]), in_tiles(lambda ct: basis[ct, mine_x, 0]),
        in_tiles(lambda ct: basis[ct, core * (depth - 1)]),
    ], axis=0)
    those = jnp.concatenate([
        coefficients[CORES * x + k].reshape(narrow * owned, modes).astype(bf16)
        for k in range(CORES) for x in range(chips)
    ], axis=0)
    on_edge = dot(own_edge, those, NT).astype(bf16)
    for k in range(CORES):
        edge_out[k] = on_edge[:, k * narrow * unit:(k + 1) * narrow * unit]
    send_all(edges)
    send_all(faces)

    def arrange(first, values, keep):
        count = values.shape[0]
        if keep:
            rows_of[pl.ds(first, count), :] = values
        columns_of[:, pl.ds(first, count)] = values.T

    arrange(pl.multiple_of(core * half, half), in_tiles(lambda ct: basis[ct, mine_x]), True)

    speeds.wait()
    own_kappa.wait()
    for k in range(3):
        speed[k] = (0.25 * jnp.broadcast_to(velocity[k:k + 1, :], (LANES, samples))).T

    all_in_go_on()
    mate_back.wait_recv()
    mate_kappa.wait_recv()
    arrange(pl.multiple_of((1 - core) * half, half), in_tiles(lambda ct: basis[ct, theirs_x]), True)

    def rounded(rows, at):
        return dot(rows, columns_of[:, at], NN).astype(bf16).astype(f32)

    first_rows = jnp.concatenate([
        coefficients[CORES * peer(chip, e ^ far_x) + core, peer(me_n, d ^ far_n)].astype(bf16)
        for d in range(narrow) for e in range(chips)
    ], axis=0)
    inner = slice(0, cells)
    field[:, inner] = rounded(first_rows, inner)

    cell = lax.broadcasted_iota(jnp.int32, (1, cells), 1)
    y_of, z_of = (cell % pitch) // size_z, cell % size_z
    pick = (y_of == lax.broadcasted_iota(jnp.int32, (size_y, cells), 0)).astype(bf16)
    line = lax.broadcasted_iota(jnp.int32, (depth * size_z, cells), 0)
    own_row = (line == (cell // pitch) * size_z + z_of).astype(f32)
    rest = kappa[...].reshape(depth * size_z, size_y)
    found = jnp.zeros((depth * size_z, cells), f32)
    for _ in range(3):
        part = rest.astype(bf16)
        rest = rest - part.astype(f32)
        found = found + dot(part, pick, NN)
    factor[...] = jnp.broadcast_to(jnp.sum(found * own_row, axis=0, keepdims=True), factor.shape)

    take_all(edges)
    for k in range(edge_of.shape[0]):
        edge_of[k] = edge_in[k * LANES:(k + 1) * LANES, :].T.astype(f32)

    lane = lax.broadcasted_iota(jnp.int32, (8, LANES), 1)
    lane_x, lane_y, lane_z = lane // pitch, (lane % pitch) // size_z, lane % size_z
    per_tile = LANES // pitch
    low_y, high_y = lane_y == 0, lane_y == size_y - 1
    first_of_tile, last_of_tile = lane < pitch, lane >= LANES - pitch
    from_border = lane_x * size_z + lane_z + jnp.where(high_y, y_rows * size_z, 0)
    z_sign = jnp.where(lane_z == 0, 1.0, -1.0)

    def stencil(first, speeds_of, edge_rows):
        def at(t):
            if t >= tiles and edge_rows:
                return joined([edge_of[t - tiles, pl.ds(row, count), :] for row in edge_rows])
            return field[first:first + 8, t * LANES:(t + 1) * LANES]

        def turn(value, by):
            return pltpu.roll(value, by % LANES, 1)

        v_x, v_y, v_z = speeds_of
        if size_z == 2:
            v_z = v_z * z_sign
        center = [at(t) for t in range(tiles + 1)]
        ahead = [turn(value, -pitch) for value in center]
        behind = [turn(value, pitch) for value in center]
        y_border = at(tiles + 1)
        out = []
        for t in range(tiles):
            mid = center[t]
            x_next = jnp.where(last_of_tile, ahead[t + 1], ahead[t])
            x_prev = jnp.where(first_of_tile, behind[t - 1], behind[t])
            outside = jnp.take_along_axis(y_border, from_border + t * per_tile * size_z, axis=1)
            y_next = jnp.where(high_y, outside, turn(mid, -size_z))
            y_prev = jnp.where(low_y, outside, turn(mid, size_z))
            x_sum, y_sum = x_next + x_prev, y_next + y_prev
            carried = v_x * (x_sum * (x_next - x_prev)) + v_y * (y_sum * (y_next - y_prev))
            if size_z == 2:
                z_sum = jnp.where(lane_z == 0, turn(mid, -1), turn(mid, 1))
                carried = carried + v_z * (z_sum * z_sum)
            else:
                z_next = jnp.where(lane_z < size_z - 1, turn(mid, -1), 0.0)
                z_prev = jnp.where(lane_z > 0, turn(mid, 1), 0.0)
                z_sum = z_next + z_prev
                carried = carried + v_z * (z_sum * (z_next - z_prev))
            spread = x_sum + y_sum + z_sum - 6.0 * mid
            out.append(factor[:, t * LANES:(t + 1) * LANES] * spread - carried)
        return jnp.concatenate(out, axis=1)

    count = min(8, owned)

    def joined(pieces):
        return jnp.concatenate(pieces, axis=0) if len(pieces) > 1 else pieces[0]

    def places(first):
        for row in range(first, first + 8, count):
            d, e, inner = row // unit, row % unit // owned, row % owned
            x, n = peer(chip, e ^ far_x), peer(me_n, d ^ far_n)
            pair = (x * narrow + n) * owned + inner, ((CORES * x + core) * narrow + n) * owned + inner
            yield tuple(pl.multiple_of(at, 8) for at in pair) if count == 8 else pair

    def speeds_at(first):
        rows = [at for _, at in places(first)]
        return [joined([speed[k, pl.ds(at, count), :] for at in rows]) for k in range(3)]

    def slot(d, e):
        return d * chips + e - 1

    def scatter(group, step, residue):
        made = []
        for first in rows_in(group):
            edge_rows = [at for at, _ in places(first)] if step == 0 else []
            made.append(stencil(first, speeds_at(first), edge_rows))
        total = dot(jnp.concatenate(made, axis=0).astype(bf16), rows_of[...], NN)
        copies = []
        for i, (d, e) in enumerate(group):
            block = total[i * owned:(i + 1) * owned]
            if step == ITERS - 1 and d + e == 0 and far_n + far_x > 0:
                block = block + residue * (1.0 / (step_size * scale))
            to_n, to_x = (d ^ far_n, e ^ far_x) if step == ITERS - 1 else (d, e)
            if to_n + to_x == 0:
                kept[...] = block
                continue
            at = slot(to_n, to_x)
            reduced[at] = block.astype(WIRE)
            copies.append(remote(
                reduced.at[at], landed.at[step, at], r_send, r_recv.at[step],
                CORES * peer(chip, to_x) + core, peer(me_n, to_n),
            ))
        return copies

    def each(there):
        for d in range(narrow):
            for e in range(chips):
                if d + e > 0:
                    there(d, e)

    def reduced_sent():
        arrival(reduced, r_send, r_recv.at[0]).wait_send()

    def mine_sent():
        arrival(reduced, g_send, r_recv.at[0]).wait_send()

    blocks_of = [[(d, e) for e in reversed(range(chips))] for d in range(narrow)]
    nearer, farther = range(narrow // 2), range(narrow // 2, narrow)
    if owned % 8 == 0:
        far_first = [blocks_of[d] for d in reversed(farther)]
        far_first.append(sum((blocks_of[d] for d in reversed(nearer)), []))
        near_first = [[(0, 0)], [(0, e) for e in range(1, chips)]]
        near_first += [blocks_of[d][::-1] for d in nearer if d > 0]
        near_first.append(sum((blocks_of[d][::-1] for d in farther), []))
        near_first = [group for group in near_first if group]
    else:
        far_first = [sum((blocks_of[d][::-1] for d in part), []) for part in (farther, nearer)]
        near_first = far_first[::-1]

    def rows_in(group):
        if owned % 8 == 0:
            return [(d * chips + e) * owned + inner for d, e in group for inner in range(0, owned, 8)]
        return range(group[0][0] * unit, (group[-1][0] + 1) * unit, 8)

    state = coefficients[CORES * peer(chip, far_x) + core, peer(me_n, far_n)]
    residue = None
    for step in range(ITERS):
        if step > 0:
            reduced_sent()
        for number, group in enumerate(near_first if step else far_first):
            if step > 0:
                for d in sorted({d for d, e in group if d > 0 or e > 0}):
                    beyond = gathered.at[d] if d > 0 else gathered.at[0, pl.ds(1, chips - 1)]
                    arrival(beyond, g_send, g_recv.at[d]).wait_recv()
                rows = jnp.concatenate([gathered[d, e] if d + e > 0 else mine[...] for d, e in group], axis=0)
                made = rounded(rows, slice(None))
                for i, (d, e) in enumerate(group):
                    at = (d * chips + e) * owned
                    field[at:at + owned, :] = made[i * owned:(i + 1) * owned]
            copies = scatter(group, step, residue)
            if step == 0 and number == 0:
                all_in()
            for copy in copies:
                copy.start()

        if step == 0:
            take_all(faces)
            arrange(cells, in_tiles(lambda ct: border[ct]), False)
            inverse.wait()
            high = propagator[...].astype(bf16)
            g_high[...] = high.T
            g_low[...] = (propagator[...] - high.astype(f32)).astype(bf16).T

        arrival(landed.at[step], r_send, r_recv.at[step]).wait_recv()
        parts = [kept[...]]
        each(lambda d, e: parts.append(landed[step, slot(d, e)].astype(f32)))
        summed = sum(parts[1:], parts[0])

        if step == ITERS - 1 and far_n + far_x > 0:
            state = gathered[far_n, far_x].astype(f32)
        update = state + step_size * (summed * scale)
        high = update.astype(bf16)
        low = (update - high.astype(f32)).astype(bf16)
        both = dot(jnp.concatenate([high, low], axis=0), g_high[...], NN)
        small = both[owned:] + dot(high, g_low[...], NN)
        state = update + (both[:owned] + small)

        if step + 1 < ITERS:
            if step > 0:
                mine_sent()
            mine[...] = state.astype(bf16)
            residue = state - state.astype(bf16).astype(f32)
            for d in [*reversed(nearer), *reversed(farther)]:
                for e in reversed(range(chips)):
                    if d + e > 0:
                        remote(
                            mine, gathered.at[d, e], g_send, g_recv.at[d],
                            CORES * peer(chip, e) + core, peer(me_n, d),
                        ).start()

    out_ref[...] = state
    reduced_sent()
    mine_sent()
    for parts, sends, gone, comes in faces + edges:
        pl.when(sends)(gone.wait_send)
    mate_gone.wait_send()
    mate_kappa.wait_send()


def body(basis, kappa, velocity, coefficients, propagator):
    size_x, size_y, size_z, modes = basis.shape
    samples = coefficients.shape[0]
    wide, narrow = lax.axis_size("wide"), lax.axis_size("narrow")
    chips = wide // CORES
    owned = samples // (wide * narrow)
    unit = chips * owned
    scale = 1.0 / math.sqrt(size_x * size_y * size_z * wide * narrow)
    pitch = size_y * size_z
    depth = CORES * size_x
    cells = depth * pitch
    assert LANES % pitch == 0 and cells % LANES == 0 and 2 * pitch <= LANES
    assert 2 * depth * size_z == LANES and unit % 8 == 0
    border = 2 * LANES // size_z
    dma = pltpu.SemaphoreType.DMA
    hbm = pl.BlockSpec(memory_space=pltpu.HBM)
    inputs = (
        basis, kappa.transpose(0, 2, 1), velocity,
        coefficients.reshape(wide, narrow, owned, modes), propagator,
    )
    return pl.pallas_call(
        functools.partial(kernel, chips, narrow, scale),
        out_shape=jax.ShapeDtypeStruct((owned, modes), f32),
        in_specs=[hbm] * len(inputs),
        out_specs=pl.BlockSpec(memory_space=pltpu.VMEM),
        scratch_shapes=[
            pltpu.VMEM((modes // LANES, depth, size_y, size_z, LANES), bf16),
            pltpu.VMEM((modes // LANES, border, size_z, LANES), bf16),
            pltpu.VMEM((CORES, size_x, size_z, size_y), f32),
            pltpu.VMEM((3, samples), f32),
            pltpu.VMEM((wide, narrow, owned, modes), f32),
            pltpu.VMEM((modes, modes), f32),
            pltpu.VMEM((CORES, (2 * size_x + size_y) * size_z, narrow * unit), bf16),
            pltpu.VMEM((border * size_z, narrow * unit), bf16),
            pltpu.VMEM((border * size_z // LANES, narrow * unit, LANES), f32),
            pltpu.VMEM((cells, modes), bf16),
            pltpu.VMEM((modes, cells + border * size_z), bf16),
            pltpu.VMEM((narrow * unit, cells + border * size_z), f32),
            pltpu.VMEM((8, cells), f32),
            pltpu.VMEM((3, samples, LANES), f32),
            pltpu.VMEM((modes, modes), bf16),
            pltpu.VMEM((modes, modes), bf16),
            pltpu.VMEM((narrow * chips - 1, owned, modes), WIRE),
            pltpu.VMEM((ITERS, narrow * chips - 1, owned, modes), WIRE),
            pltpu.VMEM((owned, modes), f32),
            pltpu.VMEM((owned, modes), bf16),
            pltpu.VMEM((narrow, chips, owned, modes), bf16),
            dma((5,)), dma((2,)), dma((4,)), dma((5,)), dma, dma((ITERS,)), dma, dma((narrow,)), dma((3,)), dma((4,)),
            pltpu.SemaphoreType.REGULAR((4 if chips > 2 else 2,)),
        ],
        compiler_params=pltpu.CompilerParams(
            collective_id=0, has_side_effects=True, vmem_limit_bytes=48 * 1024 * 1024
        ),
    )(*(pltpu.with_memory_space_constraint(value, pltpu.HBM) for value in inputs))


def solution(mesh):
    placed = (
        P(("groups", "wide"), "narrow", None, None),
        P(("groups", "wide"), "narrow", None),
        P(None, "groups"),
        P("groups", None),
        P("groups", None),
    )
    return jax.shard_map(
        body,
        mesh=mesh,
        in_specs=placed,
        out_specs=P(("groups", "wide", "narrow"), None),
        check_vma=False,
    )
```

```python
import functools
import math

import jax
import jax.numpy as jnp
from jax import lax
from jax.experimental import pallas as pl
from jax.experimental.pallas import tpu as pltpu
from jax.sharding import PartitionSpec as P

ITERS = 2
WIRE = jnp.bfloat16
LANES = 128
CORES = 2

step_size = 4.0

NT = (((1,), (1,)), ((), ()))
NN = (((1,), (0,)), ((), ()))
f32, bf16 = jnp.float32, jnp.bfloat16


def peer(me, offset):
    result, bit = me, 1
    while bit <= offset:
        if offset & bit:
            result = result + (1 - 2 * ((me // bit) % 2)) * bit
        bit *= 2
    return result


def dot(a, b, dims):
    return lax.dot_general(a, b, dims, preferred_element_type=f32)


def kernel(
    chips, narrow, scale,
    basis_hbm, kappa_hbm, velocity_hbm, coefficients_hbm, propagator_hbm, out_ref,
    basis, border, kappa, velocity, coefficients, propagator,
    own_rows, edge_out, edge_in, edge_of, rows_of, columns_of, field, factor, speed, g_high, g_low,
    reduced, landed, kept, mine, gathered,
    load_sem, mate_recv, face_recv, out_send,
    first_recv, edge_send, edge_recv, word,
):
    r_send, g_send, g_recv = edge_send.at[0], edge_send.at[1], edge_recv
    r_recv = [first_recv] + [mate_recv.at[k] for k in range(ITERS - 1)]
    size_x, size_y, size_z, modes = basis_hbm.shape
    slices, depth = basis.shape[:2]
    owned = coefficients.shape[2]
    samples = velocity.shape[1]
    unit = chips * owned
    pitch = size_y * size_z
    half, cells = size_x * pitch, depth * pitch
    tiles = cells // LANES
    x_rows, y_rows = size_y, depth
    y_base = border.shape[1] - 2 * y_rows
    x_base = (y_base - x_rows, 0)
    wide = chips * CORES
    me_w, me_n = lax.axis_index("wide"), lax.axis_index("narrow")
    chip, core = me_w // CORES, me_w % CORES
    far_x, far_n = chips // 2, narrow // 2

    def lanes_of(ct):
        return pl.ds(ct * LANES, LANES)

    mine_x, theirs_x = pl.ds(core * size_x, size_x), pl.ds((1 - core) * size_x, size_x)
    started = pltpu.make_async_copy(coefficients_hbm, coefficients, load_sem.at[3])
    started.start()
    outer_rows = pltpu.make_async_copy(own_rows, own_rows, load_sem.at[2])
    for ct in range(slices):
        for first, count, face in (
            (0, size_x, basis_hbm.at[:, size_y - 1, :, lanes_of(ct)]),
            (size_x, size_x, basis_hbm.at[:, 0, :, lanes_of(ct)]),
            (2 * size_x, size_y, basis_hbm.at[core * (size_x - 1), :, :, lanes_of(ct)]),
        ):
            pltpu.make_async_copy(face, own_rows.at[ct, pl.ds(first, count)], load_sem.at[2]).start()
    loads = [
        pltpu.make_async_copy(basis_hbm.at[:, :, :, lanes_of(ct)], basis.at[ct, mine_x], load_sem.at[0])
        for ct in range(slices)
    ]
    loaded = pltpu.make_async_copy(basis.at[:, mine_x], basis.at[:, mine_x], load_sem.at[0])
    for load in loads:
        load.start()
    own_kappa = pltpu.make_async_copy(kappa_hbm, kappa.at[core], load_sem.at[1])
    own_kappa.start()
    speeds = pltpu.make_async_copy(velocity_hbm, velocity, load_sem.at[4])
    speeds.start()
    inverse = pltpu.make_async_copy(propagator_hbm, propagator, load_sem.at[3])


    barrier = pltpu.get_barrier_semaphore()

    def greet(w, n):
        pl.semaphore_signal(
            barrier, inc=1, device_id={"wide": w, "narrow": n}, device_id_type=pl.DeviceIdType.MESH
        )

    greet(peer(me_w, 1), me_n)
    greetings = 1
    for step in (-1, 1):
        n, x = me_n + step, chip + step
        n_there = jnp.logical_and(n >= 0, n < narrow)
        x_there = jnp.logical_and(x >= 0, x < chips)

        def along_narrow(n=n):
            for k in range(CORES):
                greet(peer(me_w, k), n)

        def along_wide(x=x):
            for k in range(CORES):
                greet(CORES * x + k, me_n)

        pl.when(n_there)(along_narrow)
        pl.when(x_there)(along_wide)
        greetings = greetings + CORES * (jnp.where(n_there, 1, 0) + jnp.where(x_there, 1, 0))

    def clear(first, count):
        border[:, pl.ds(first, count)] = jnp.zeros((slices, count) + border.shape[2:], bf16)
        at = slice(first * size_z, (first + count) * size_z)
        edge_in[at, :] = jnp.zeros((count * size_z, edge_in.shape[1]), bf16)

    pl.when(chip == 0)(lambda: clear(x_base[0], x_rows))
    pl.when(chip == chips - 1)(lambda: clear(x_base[1], x_rows))
    pl.when(me_n == 0)(lambda: clear(y_base, y_rows))
    pl.when(me_n == narrow - 1)(lambda: clear(y_base + y_rows, y_rows))

    pl.semaphore_wait(barrier, greetings)

    def lines(count, at, where, forth, back):
        def tell(sem, step):
            pl.semaphore_signal(
                sem, inc=1, device_id=where(at + step), device_id_type=pl.DeviceIdType.MESH
            )

        def begin():
            pl.when(at == 0)(lambda: tell(forth, 1))
            pl.when(at == count - 1)(lambda: tell(back, -1))

        def pass_on(sem, step):
            pl.semaphore_wait(sem, 1)
            tell(sem, step)

        def from_ends():
            if count > 2:
                pl.when(at == 1)(lambda: pass_on(forth, 1))
                pl.when(at == count - 2)(lambda: pass_on(back, -1))

        def go_on():
            if count > 3:
                pl.when(jnp.logical_and(at > 1, at < count - 1))(lambda: pass_on(forth, 1))
                pl.when(jnp.logical_and(at > 0, at < count - 2))(lambda: pass_on(back, -1))

        def end():
            pl.when(at == count - 1)(lambda: pl.semaphore_wait(forth, 1))
            pl.when(at == 0)(lambda: pl.semaphore_wait(back, 1))

        return begin, from_ends, go_on, end

    if chips > 2:
        for phase in lines(
            chips, chip, lambda x: {"wide": CORES * x + core, "narrow": me_n}, word.at[2], word.at[3]
        ):
            phase()
    all_in_begin, all_in_from_ends, all_in_go_on, all_in = lines(
        narrow, me_n, lambda n: {"wide": me_w, "narrow": n}, word.at[0], word.at[1]
    )
    all_in_begin()

    def remote(src, dst, send, recv, w, n):
        return pltpu.make_async_remote_copy(
            src_ref=src, dst_ref=dst, send_sem=send, recv_sem=recv,
            device_id={"wide": w, "narrow": n}, device_id_type=pl.DeviceIdType.MESH,
        )

    def arrival(ref, send, recv):
        return remote(ref, ref, send, recv, me_w, me_n)

    faces, edges = [], []
    line_x, line_y = size_y * size_z, size_x * size_z

    def edge(face, first, count, number, came, w, n):
        parts = [
            remote(
                edge_out.at[k, pl.ds(face[0], face[1])], edge_in.at[pl.ds(first, count)],
                edge_send.at[number], edge_recv.at[came], w(k), n,
            )
            for k in range(CORES)
        ]
        gone = arrival(edge_in.at[pl.ds(0, CORES * count)], edge_send.at[number], edge_recv.at[came])
        return parts, gone

    def whole_edge(first, count, number):
        return arrival(edge_in.at[pl.ds(first * size_z, count * size_z)], edge_send.at[0], edge_recv.at[number])

    for j, (from_y, step) in enumerate(((size_y - 1, 1), (0, -1))):
        n = lax.rem(me_n + step + narrow, narrow)
        first = y_base + j * y_rows
        parts = [
            remote(
                basis_hbm.at[:, from_y, :, lanes_of(ct)], border.at[ct, pl.ds(first + core * size_x, size_x)],
                out_send.at[j], face_recv.at[j], peer(me_w, k), n,
            )
            for k in range(CORES) for ct in range(slices)
        ]
        came = arrival(border.at[:, pl.ds(first, y_rows)], out_send.at[j], face_recv.at[j])
        goes = jnp.logical_and(me_n + step >= 0, me_n + step < narrow)
        there = jnp.logical_and(me_n - step >= 0, me_n - step < narrow)
        faces.append((parts, goes, came, [(came, there)]))
        at = pl.multiple_of(first * size_z + core * line_y, line_y)
        parts, gone = edge((j * line_y, line_y), at, line_y, j, j, lambda k: CORES * chip + k, n)
        edges.append((parts, goes, gone, [(whole_edge(first, y_rows, j), there)]))
    toward = chip + 2 * core - 1
    x_to = lax.rem(toward + chips, chips)
    parts = [
        remote(
            basis_hbm.at[core * (size_x - 1), :, :, lanes_of(ct)], border.at[ct, pl.ds(core * x_base[0], x_rows)],
            out_send.at[2], face_recv.at[2 + core], CORES * x_to + k, me_n,
        )
        for k in range(CORES) for ct in range(slices)
    ]
    goes = jnp.logical_and(toward >= 0, toward < chips)
    faces.append((
        parts, goes,
        arrival(border.at[:, pl.ds(0, CORES * x_rows)], out_send.at[2], face_recv.at[2]),
        [
            (arrival(border.at[:, pl.ds(k * x_base[0], x_rows)], out_send.at[2], face_recv.at[2 + k]), there)
            for k, there in ((0, chip < chips - 1), (1, chip > 0))
        ],
    ))
    at = pl.multiple_of(core * (x_base[0] * size_z), line_x)
    parts, gone = edge((2 * line_y, line_x), at, line_x, 2, 2 + core, lambda k: CORES * x_to + k, me_n)
    edges.append((parts, goes, gone, [
        (whole_edge(k * x_base[0], x_rows, 2 + k), there) for k, there in ((0, chip < chips - 1), (1, chip > 0))
    ]))

    def send_all(copies):
        for parts, sends, gone, comes in copies:
            def go(parts=parts):
                for part in parts:
                    part.start()
            pl.when(sends)(go)

    def take_all(copies):
        for parts, sends, gone, comes in copies:
            for came, there in comes:
                pl.when(there)(came.wait_recv)

    mate = [
        remote(
            basis_hbm.at[:, :, :, lanes_of(ct)], basis.at[ct, mine_x],
            out_send.at[3], mate_recv.at[0], peer(me_w, 1), me_n,
        )
        for ct in range(slices)
    ]
    mate_gone = arrival(basis.at[:, mine_x], out_send.at[3], mate_recv.at[0])
    mate_back = arrival(basis.at[:, theirs_x], out_send.at[3], mate_recv.at[0])
    mate_kappa = remote(kappa_hbm, kappa.at[core], out_send.at[4], mate_recv.at[1], peer(me_w, 1), me_n)

    started.wait()
    outer_rows.wait()

    def in_tiles(of):
        return jnp.concatenate([of(ct).reshape(-1, LANES) for ct in range(slices)], axis=1)

    own_edge = in_tiles(lambda ct: own_rows[ct])
    those = jnp.concatenate([
        coefficients[CORES * x + k].reshape(narrow * owned, modes).astype(bf16)
        for k in range(CORES) for x in range(chips)
    ], axis=0)
    on_edge = dot(own_edge, those, NT).astype(bf16)
    for k in range(CORES):
        edge_out[k] = on_edge[:, k * narrow * unit:(k + 1) * narrow * unit]
    send_all(edges)
    for part in mate:
        part.start()
    mate_kappa.start()
    send_all(faces)

    def arrange(first, values, keep):
        count = values.shape[0]
        if keep:
            rows_of[pl.ds(first, count), :] = values
        columns_of[:, pl.ds(first, count)] = values.T

    loaded.wait()
    inverse.start()
    arrange(pl.multiple_of(core * half, half), in_tiles(lambda ct: basis[ct, mine_x]), True)

    speeds.wait()
    own_kappa.wait()
    for k in range(3):
        speed[k] = (0.25 * jnp.broadcast_to(velocity[k:k + 1, :], (LANES, samples))).T

    all_in_from_ends()
    mate_back.wait_recv()
    mate_kappa.wait_recv()
    arrange(pl.multiple_of((1 - core) * half, half), in_tiles(lambda ct: basis[ct, theirs_x]), True)

    def rounded(rows, at):
        return dot(rows, columns_of[:, at], NN).astype(bf16).astype(f32)

    first_rows = jnp.concatenate([
        coefficients[CORES * peer(chip, e ^ far_x) + core, peer(me_n, d ^ far_n)].astype(bf16)
        for d in range(narrow) for e in range(chips)
    ], axis=0)
    inner = slice(0, cells)
    field[:, inner] = rounded(first_rows, inner)

    cell = lax.broadcasted_iota(jnp.int32, (1, cells), 1)
    y_of, z_of = (cell % pitch) // size_z, cell % size_z
    pick = (y_of == lax.broadcasted_iota(jnp.int32, (size_y, cells), 0)).astype(bf16)
    line = lax.broadcasted_iota(jnp.int32, (depth * size_z, cells), 0)
    own_row = (line == (cell // pitch) * size_z + z_of).astype(f32)
    rest = kappa[...].reshape(depth * size_z, size_y)
    found = jnp.zeros((depth * size_z, cells), f32)
    for _ in range(3):
        part = rest.astype(bf16)
        rest = rest - part.astype(f32)
        found = found + dot(part, pick, NN)
    factor[...] = jnp.broadcast_to(jnp.sum(found * own_row, axis=0, keepdims=True), factor.shape)

    all_in_go_on()
    take_all(edges)
    for k in range(edge_of.shape[0]):
        edge_of[k] = edge_in[k * LANES:(k + 1) * LANES, :].T.astype(f32)

    lane = lax.broadcasted_iota(jnp.int32, (8, LANES), 1)
    lane_x, lane_y, lane_z = lane // pitch, (lane % pitch) // size_z, lane % size_z
    per_tile = LANES // pitch
    low_y, high_y = lane_y == 0, lane_y == size_y - 1
    first_of_tile, last_of_tile = lane < pitch, lane >= LANES - pitch
    from_border = lane_x * size_z + lane_z + jnp.where(high_y, y_rows * size_z, 0)
    z_sign = jnp.where(lane_z == 0, 1.0, -1.0)

    def stencil(first, speeds_of, edge_rows):
        def at(t):
            if t >= tiles and edge_rows:
                return joined([edge_of[t - tiles, pl.ds(row, count), :] for row in edge_rows])
            return field[first:first + 8, t * LANES:(t + 1) * LANES]

        def turn(value, by):
            return pltpu.roll(value, by % LANES, 1)

        v_x, v_y, v_z = speeds_of
        if size_z == 2:
            v_z = v_z * z_sign
        center = [at(t) for t in range(tiles + 1)]
        ahead = [turn(value, -pitch) for value in center]
        behind = [turn(value, pitch) for value in center]
        y_border = at(tiles + 1)
        out = []
        for t in range(tiles):
            mid = center[t]
            x_next = jnp.where(last_of_tile, ahead[t + 1], ahead[t])
            x_prev = jnp.where(first_of_tile, behind[t - 1], behind[t])
            outside = jnp.take_along_axis(y_border, from_border + t * per_tile * size_z, axis=1)
            y_next = jnp.where(high_y, outside, turn(mid, -size_z))
            y_prev = jnp.where(low_y, outside, turn(mid, size_z))
            x_sum, y_sum = x_next + x_prev, y_next + y_prev
            carried = v_x * (x_sum * (x_next - x_prev)) + v_y * (y_sum * (y_next - y_prev))
            if size_z == 2:
                z_sum = jnp.where(lane_z == 0, turn(mid, -1), turn(mid, 1))
                carried = carried + v_z * (z_sum * z_sum)
            else:
                z_next = jnp.where(lane_z < size_z - 1, turn(mid, -1), 0.0)
                z_prev = jnp.where(lane_z > 0, turn(mid, 1), 0.0)
                z_sum = z_next + z_prev
                carried = carried + v_z * (z_sum * (z_next - z_prev))
            spread = x_sum + y_sum + z_sum - 6.0 * mid
            out.append(factor[:, t * LANES:(t + 1) * LANES] * spread - carried)
        return jnp.concatenate(out, axis=1)

    count = min(8, owned)

    def joined(pieces):
        return jnp.concatenate(pieces, axis=0) if len(pieces) > 1 else pieces[0]

    def places(first):
        for row in range(first, first + 8, count):
            d, e, inner = row // unit, row % unit // owned, row % owned
            x, n = peer(chip, e ^ far_x), peer(me_n, d ^ far_n)
            pair = (x * narrow + n) * owned + inner, ((CORES * x + core) * narrow + n) * owned + inner
            yield tuple(pl.multiple_of(at, 8) for at in pair) if count == 8 else pair

    def speeds_at(first):
        rows = [at for _, at in places(first)]
        return [joined([speed[k, pl.ds(at, count), :] for at in rows]) for k in range(3)]

    def slot(d, e):
        return d * chips + e - 1

    def scatter(group, step, residue):
        made = []
        for first in rows_in(group):
            edge_rows = [at for at, _ in places(first)] if step == 0 else []
            made.append(stencil(first, speeds_at(first), edge_rows))
        total = dot(jnp.concatenate(made, axis=0).astype(bf16), rows_of[...], NN)
        copies = []
        for i, (d, e) in enumerate(group):
            block = total[i * owned:(i + 1) * owned]
            if step == ITERS - 1 and d + e == 0 and far_n + far_x > 0:
                block = block + residue * (1.0 / (step_size * scale))
            to_n, to_x = (d ^ far_n, e ^ far_x) if step == ITERS - 1 else (d, e)
            if to_n + to_x == 0:
                kept[...] = block
                continue
            at = slot(to_n, to_x)
            reduced[at] = block.astype(WIRE)
            copies.append(remote(
                reduced.at[at], landed.at[step, at], r_send, r_recv[step],
                CORES * peer(chip, to_x) + core, peer(me_n, to_n),
            ))
        return copies

    def each(there):
        for d in range(narrow):
            for e in range(chips):
                if d + e > 0:
                    there(d, e)

    def reduced_sent():
        arrival(reduced, r_send, r_recv[0]).wait_send()

    def mine_sent():
        arrival(reduced, g_send, r_recv[0]).wait_send()

    blocks_of = [[(d, e) for e in reversed(range(chips))] for d in range(narrow)]
    nearer, farther = range(narrow // 2), range(narrow // 2, narrow)
    if owned % 8 == 0:
        far_first = [blocks_of[d] for d in reversed(farther)]
        far_first.append(sum((blocks_of[d] for d in reversed(nearer)), []))
        near_first = [[(0, 0)], [(0, e) for e in range(1, chips)]]
        near_first += [blocks_of[d][::-1] for d in nearer if d > 0]
        near_first.append(sum((blocks_of[d][::-1] for d in farther), []))
        near_first = [group for group in near_first if group]
    else:
        far_first = [sum((blocks_of[d][::-1] for d in part), []) for part in (farther, nearer)]
        near_first = far_first[::-1]

    def rows_in(group):
        if owned % 8 == 0:
            return [(d * chips + e) * owned + inner for d, e in group for inner in range(0, owned, 8)]
        return range(group[0][0] * unit, (group[-1][0] + 1) * unit, 8)

    state = coefficients[CORES * peer(chip, far_x) + core, peer(me_n, far_n)]
    residue = None
    for step in range(ITERS):
        if step > 0:
            reduced_sent()
        for number, group in enumerate(near_first if step else far_first):
            if step > 0:
                for d in sorted({d for d, e in group if d > 0 or e > 0}):
                    beyond = gathered.at[d] if d > 0 else gathered.at[0, pl.ds(1, chips - 1)]
                    arrival(beyond, g_send, g_recv.at[d]).wait_recv()
                rows = jnp.concatenate([gathered[d, e] if d + e > 0 else mine[...] for d, e in group], axis=0)
                made = rounded(rows, slice(None))
                for i, (d, e) in enumerate(group):
                    at = (d * chips + e) * owned
                    field[at:at + owned, :] = made[i * owned:(i + 1) * owned]
            parts = [group]
            if step > 0 and group is near_first[-1] and owned % 8 == 0 and len(group) > 1:
                parts = [group[len(group) // 2:], group[:len(group) // 2]]
            for part in parts:
                copies = scatter(part, step, residue)
                if step == 0 and number == 0:
                    for pieces, sends, gone, comes in edges:
                        pl.when(sends)(gone.wait_send)
                    all_in()
                for copy in copies:
                    copy.start()

        if step == 0:
            take_all(faces)
            arrange(cells, in_tiles(lambda ct: border[ct]), False)
            inverse.wait()
            high = propagator[...].astype(bf16)
            g_high[...] = high.T
            g_low[...] = (propagator[...] - high.astype(f32)).astype(bf16).T

        arrival(landed.at[step], r_send, r_recv[step]).wait_recv()
        parts = [kept[...]]
        each(lambda d, e: parts.append(landed[step, slot(d, e)].astype(f32)))
        summed = sum(parts[1:], parts[0])

        if step == ITERS - 1 and far_n + far_x > 0:
            state = gathered[far_n, far_x].astype(f32)
        update = state + step_size * (summed * scale)
        high = update.astype(bf16)
        low = (update - high.astype(f32)).astype(bf16)
        both = dot(jnp.concatenate([high, low], axis=0), g_high[...], NN)
        small = both[owned:] + dot(high, g_low[...], NN)
        state = update + (both[:owned] + small)

        if step + 1 < ITERS:
            if step > 0:
                mine_sent()
            mine[...] = state.astype(bf16)
            residue = state - state.astype(bf16).astype(f32)
            for d in [*reversed(nearer), *reversed(farther)]:
                for e in reversed(range(chips)):
                    if d + e > 0:
                        remote(
                            mine, gathered.at[d, e], g_send, g_recv.at[d],
                            CORES * peer(chip, e) + core, peer(me_n, d),
                        ).start()

    out_ref[...] = state
    reduced_sent()
    mine_sent()
    for parts, sends, gone, comes in faces:
        pl.when(sends)(gone.wait_send)
    mate_gone.wait_send()
    mate_kappa.wait_send()


def body(basis, kappa, velocity, coefficients, propagator):
    size_x, size_y, size_z, modes = basis.shape
    samples = coefficients.shape[0]
    wide, narrow = lax.axis_size("wide"), lax.axis_size("narrow")
    chips = wide // CORES
    owned = samples // (wide * narrow)
    unit = chips * owned
    scale = 1.0 / math.sqrt(size_x * size_y * size_z * wide * narrow)
    pitch = size_y * size_z
    depth = CORES * size_x
    cells = depth * pitch
    assert LANES % pitch == 0 and cells % LANES == 0 and 2 * pitch <= LANES
    assert 2 * depth * size_z == LANES and unit % 8 == 0
    border = 2 * LANES // size_z
    dma = pltpu.SemaphoreType.DMA
    hbm = pl.BlockSpec(memory_space=pltpu.HBM)
    inputs = (
        basis, kappa.transpose(0, 2, 1), velocity,
        coefficients.reshape(wide, narrow, owned, modes), propagator,
    )
    return pl.pallas_call(
        functools.partial(kernel, chips, narrow, scale),
        out_shape=jax.ShapeDtypeStruct((owned, modes), f32),
        in_specs=[hbm] * len(inputs),
        out_specs=pl.BlockSpec(memory_space=pltpu.VMEM),
        scratch_shapes=[
            pltpu.VMEM((modes // LANES, depth, size_y, size_z, LANES), bf16),
            pltpu.VMEM((modes // LANES, border, size_z, LANES), bf16),
            pltpu.VMEM((CORES, size_x, size_z, size_y), f32),
            pltpu.VMEM((3, samples), f32),
            pltpu.VMEM((wide, narrow, owned, modes), f32),
            pltpu.VMEM((modes, modes), f32),
            pltpu.VMEM((modes // LANES, 2 * size_x + size_y, size_z, LANES), bf16),
            pltpu.VMEM((CORES, (2 * size_x + size_y) * size_z, narrow * unit), bf16),
            pltpu.VMEM((border * size_z, narrow * unit), bf16),
            pltpu.VMEM((border * size_z // LANES, narrow * unit, LANES), f32),
            pltpu.VMEM((cells, modes), bf16),
            pltpu.VMEM((modes, cells + border * size_z), bf16),
            pltpu.VMEM((narrow * unit, cells + border * size_z), f32),
            pltpu.VMEM((8, cells), f32),
            pltpu.VMEM((3, samples, LANES), f32),
            pltpu.VMEM((modes, modes), bf16),
            pltpu.VMEM((modes, modes), bf16),
            pltpu.VMEM((narrow * chips - 1, owned, modes), WIRE),
            pltpu.VMEM((ITERS, narrow * chips - 1, owned, modes), WIRE),
            pltpu.VMEM((owned, modes), f32),
            pltpu.VMEM((owned, modes), bf16),
            pltpu.VMEM((narrow, chips, owned, modes), bf16),
            dma((5,)), dma((2,)), dma((4,)), dma((5,)), dma, dma((3,)), dma((max(4, narrow),)),
            pltpu.SemaphoreType.REGULAR((4 if chips > 2 else 2,)),
        ],
        compiler_params=pltpu.CompilerParams(
            collective_id=0, has_side_effects=True, vmem_limit_bytes=48 * 1024 * 1024
        ),
    )(*(pltpu.with_memory_space_constraint(value, pltpu.HBM) for value in inputs))


def solution(mesh):
    placed = (
        P(("groups", "wide"), "narrow", None, None),
        P(("groups", "wide"), "narrow", None),
        P(None, "groups"),
        P("groups", None),
        P("groups", None),
    )
    return jax.shard_map(
        body,
        mesh=mesh,
        in_specs=placed,
        out_specs=P(("groups", "wide", "narrow"), None),
        check_vma=False,
    )
```

```python
import functools
import math

import jax
import jax.numpy as jnp
from jax import lax
from jax.experimental import pallas as pl
from jax.experimental.pallas import tpu as pltpu
from jax.sharding import PartitionSpec as P

ITERS = 2
WIRE = jnp.bfloat16
LANES = 128
CORES = 2

step_size = 4.0

NT = (((1,), (1,)), ((), ()))
NN = (((1,), (0,)), ((), ()))
f32, bf16 = jnp.float32, jnp.bfloat16


def peer(me, offset):
    result, bit = me, 1
    while bit <= offset:
        if offset & bit:
            result = result + (1 - 2 * ((me // bit) % 2)) * bit
        bit *= 2
    return result


def dot(a, b, dims):
    return lax.dot_general(a, b, dims, preferred_element_type=f32)


def kernel(
    chips, narrow, scale,
    basis_hbm, kappa_hbm, velocity_hbm, coefficients_hbm, propagator_hbm, out_ref,
    basis, border, kappa, velocity, coefficients, propagator,
    own_rows, edge_out, edge_in, edge_of, rows_of, columns_of, field, factor, speed, g_high, g_low,
    reduced, landed, kept, mine, gathered,
    load_sem, mate_recv, face_recv, out_send,
    first_recv, edge_send, edge_recv, word,
):
    r_send, g_send, g_recv = edge_send.at[0], edge_send.at[1], edge_recv
    r_recv = [first_recv] + [mate_recv.at[k] for k in range(ITERS - 1)]
    size_x, size_y, size_z, modes = basis_hbm.shape
    slices, depth = basis.shape[:2]
    owned = coefficients.shape[2]
    samples = velocity.shape[1]
    unit = chips * owned
    pitch = size_y * size_z
    half, cells = size_x * pitch, depth * pitch
    tiles = cells // LANES
    x_rows, y_rows = size_y, depth
    y_base = border.shape[1] - 2 * y_rows
    x_base = (y_base - x_rows, 0)
    wide = chips * CORES
    me_w, me_n = lax.axis_index("wide"), lax.axis_index("narrow")
    chip, core = me_w // CORES, me_w % CORES
    far_x, far_n = chips // 2, narrow // 2

    def lanes_of(ct):
        return pl.ds(ct * LANES, LANES)

    mine_x, theirs_x = pl.ds(core * size_x, size_x), pl.ds((1 - core) * size_x, size_x)
    started = pltpu.make_async_copy(coefficients_hbm, coefficients, load_sem.at[3])
    started.start()
    outer_rows = pltpu.make_async_copy(own_rows, own_rows, load_sem.at[2])
    for ct in range(slices):
        for first, count, face in (
            (0, size_x, basis_hbm.at[:, size_y - 1, :, lanes_of(ct)]),
            (size_x, size_x, basis_hbm.at[:, 0, :, lanes_of(ct)]),
            (2 * size_x, size_y, basis_hbm.at[core * (size_x - 1), :, :, lanes_of(ct)]),
        ):
            pltpu.make_async_copy(face, own_rows.at[ct, pl.ds(first, count)], load_sem.at[2]).start()
    loads = [
        pltpu.make_async_copy(basis_hbm.at[:, :, :, lanes_of(ct)], basis.at[ct, mine_x], load_sem.at[0])
        for ct in range(slices)
    ]
    loaded = pltpu.make_async_copy(basis.at[:, mine_x], basis.at[:, mine_x], load_sem.at[0])
    for load in loads:
        load.start()
    own_kappa = pltpu.make_async_copy(kappa_hbm, kappa.at[core], load_sem.at[1])
    own_kappa.start()
    speeds = pltpu.make_async_copy(velocity_hbm, velocity, load_sem.at[4])
    speeds.start()
    inverse = pltpu.make_async_copy(propagator_hbm, propagator, load_sem.at[3])


    barrier = pltpu.get_barrier_semaphore()

    def greet(w, n):
        pl.semaphore_signal(
            barrier, inc=1, device_id={"wide": w, "narrow": n}, device_id_type=pl.DeviceIdType.MESH
        )

    greet(peer(me_w, 1), me_n)
    greetings = 1
    for step in (-1, 1):
        n, x = me_n + step, chip + step
        n_there = jnp.logical_and(n >= 0, n < narrow)
        x_there = jnp.logical_and(x >= 0, x < chips)

        def along_narrow(n=n):
            for k in range(CORES):
                greet(peer(me_w, k), n)

        def along_wide(x=x):
            for k in range(CORES):
                greet(CORES * x + k, me_n)

        pl.when(n_there)(along_narrow)
        pl.when(x_there)(along_wide)
        greetings = greetings + CORES * (jnp.where(n_there, 1, 0) + jnp.where(x_there, 1, 0))

    def clear(first, count):
        border[:, pl.ds(first, count)] = jnp.zeros((slices, count) + border.shape[2:], bf16)
        at = slice(first * size_z, (first + count) * size_z)
        edge_in[at, :] = jnp.zeros((count * size_z, edge_in.shape[1]), bf16)

    pl.when(chip == 0)(lambda: clear(x_base[0], x_rows))
    pl.when(chip == chips - 1)(lambda: clear(x_base[1], x_rows))
    pl.when(me_n == 0)(lambda: clear(y_base, y_rows))
    pl.when(me_n == narrow - 1)(lambda: clear(y_base + y_rows, y_rows))

    pl.semaphore_wait(barrier, greetings)

    def lines(count, at, where, forth, back):
        def tell(sem, step):
            pl.semaphore_signal(
                sem, inc=1, device_id=where(at + step), device_id_type=pl.DeviceIdType.MESH
            )

        def begin():
            pl.when(at == 0)(lambda: tell(forth, 1))
            pl.when(at == count - 1)(lambda: tell(back, -1))

        def pass_on(sem, step):
            pl.semaphore_wait(sem, 1)
            tell(sem, step)

        def from_ends():
            if count > 2:
                pl.when(at == 1)(lambda: pass_on(forth, 1))
                pl.when(at == count - 2)(lambda: pass_on(back, -1))

        def go_on():
            if count > 3:
                pl.when(jnp.logical_and(at > 1, at < count - 1))(lambda: pass_on(forth, 1))
                pl.when(jnp.logical_and(at > 0, at < count - 2))(lambda: pass_on(back, -1))

        def end():
            pl.when(at == count - 1)(lambda: pl.semaphore_wait(forth, 1))
            pl.when(at == 0)(lambda: pl.semaphore_wait(back, 1))

        return begin, from_ends, go_on, end

    if chips > 2:
        for phase in lines(
            chips, chip, lambda x: {"wide": CORES * x + core, "narrow": me_n}, word.at[2], word.at[3]
        ):
            phase()
    all_in_begin, all_in_from_ends, all_in_go_on, all_in = lines(
        narrow, me_n, lambda n: {"wide": me_w, "narrow": n}, word.at[0], word.at[1]
    )
    all_in_begin()

    def remote(src, dst, send, recv, w, n):
        return pltpu.make_async_remote_copy(
            src_ref=src, dst_ref=dst, send_sem=send, recv_sem=recv,
            device_id={"wide": w, "narrow": n}, device_id_type=pl.DeviceIdType.MESH,
        )

    def arrival(ref, send, recv):
        return remote(ref, ref, send, recv, me_w, me_n)

    faces, edges = [], []
    line_x, line_y = size_y * size_z, size_x * size_z

    def edge(face, first, count, number, came, w, n):
        parts = [
            remote(
                edge_out.at[k, pl.ds(face[0], face[1])], edge_in.at[pl.ds(first, count)],
                edge_send.at[number], edge_recv.at[came], w(k), n,
            )
            for k in range(CORES)
        ]
        gone = arrival(edge_in.at[pl.ds(0, CORES * count)], edge_send.at[number], edge_recv.at[came])
        return parts, gone

    def whole_edge(first, count, number):
        return arrival(edge_in.at[pl.ds(first * size_z, count * size_z)], edge_send.at[0], edge_recv.at[number])

    for j, (from_y, step) in enumerate(((size_y - 1, 1), (0, -1))):
        n = lax.rem(me_n + step + narrow, narrow)
        first = y_base + j * y_rows
        parts = [
            remote(
                basis_hbm.at[:, from_y, :, lanes_of(ct)], border.at[ct, pl.ds(first + core * size_x, size_x)],
                out_send.at[j], face_recv.at[j], peer(me_w, k), n,
            )
            for k in range(CORES) for ct in range(slices)
        ]
        came = arrival(border.at[:, pl.ds(first, y_rows)], out_send.at[j], face_recv.at[j])
        goes = jnp.logical_and(me_n + step >= 0, me_n + step < narrow)
        there = jnp.logical_and(me_n - step >= 0, me_n - step < narrow)
        faces.append((parts, goes, came, [(came, there)]))
        at = pl.multiple_of(first * size_z + core * line_y, line_y)
        parts, gone = edge((j * line_y, line_y), at, line_y, j, j, lambda k: CORES * chip + k, n)
        edges.append((parts, goes, gone, [(whole_edge(first, y_rows, j), there)]))
    toward = chip + 2 * core - 1
    x_to = lax.rem(toward + chips, chips)
    parts = [
        remote(
            basis_hbm.at[core * (size_x - 1), :, :, lanes_of(ct)], border.at[ct, pl.ds(core * x_base[0], x_rows)],
            out_send.at[2], face_recv.at[2 + core], CORES * x_to + k, me_n,
        )
        for k in range(CORES) for ct in range(slices)
    ]
    goes = jnp.logical_and(toward >= 0, toward < chips)
    faces.append((
        parts, goes,
        arrival(border.at[:, pl.ds(0, CORES * x_rows)], out_send.at[2], face_recv.at[2]),
        [
            (arrival(border.at[:, pl.ds(k * x_base[0], x_rows)], out_send.at[2], face_recv.at[2 + k]), there)
            for k, there in ((0, chip < chips - 1), (1, chip > 0))
        ],
    ))
    at = pl.multiple_of(core * (x_base[0] * size_z), line_x)
    parts, gone = edge((2 * line_y, line_x), at, line_x, 2, 2 + core, lambda k: CORES * x_to + k, me_n)
    edges.append((parts, goes, gone, [
        (whole_edge(k * x_base[0], x_rows, 2 + k), there) for k, there in ((0, chip < chips - 1), (1, chip > 0))
    ]))

    def send_all(copies):
        for parts, sends, gone, comes in copies:
            def go(parts=parts):
                for part in parts:
                    part.start()
            pl.when(sends)(go)

    def take_all(copies):
        for parts, sends, gone, comes in copies:
            for came, there in comes:
                pl.when(there)(came.wait_recv)

    mate = [
        remote(
            basis_hbm.at[:, :, :, lanes_of(ct)], basis.at[ct, mine_x],
            out_send.at[3], mate_recv.at[0], peer(me_w, 1), me_n,
        )
        for ct in range(slices)
    ]
    mate_gone = arrival(basis.at[:, mine_x], out_send.at[3], mate_recv.at[0])
    mate_back = arrival(basis.at[:, theirs_x], out_send.at[3], mate_recv.at[0])
    mate_kappa = remote(kappa_hbm, kappa.at[core], out_send.at[4], mate_recv.at[1], peer(me_w, 1), me_n)

    started.wait()
    outer_rows.wait()

    def in_tiles(of):
        return jnp.concatenate([of(ct).reshape(-1, LANES) for ct in range(slices)], axis=1)

    own_edge = in_tiles(lambda ct: own_rows[ct])
    those = jnp.concatenate([
        coefficients[CORES * x + k].reshape(narrow * owned, modes).astype(bf16)
        for k in range(CORES) for x in range(chips)
    ], axis=0)
    on_edge = dot(own_edge, those, NT).astype(bf16)
    for k in range(CORES):
        edge_out[k] = on_edge[:, k * narrow * unit:(k + 1) * narrow * unit]
    send_all(edges)
    for part in mate:
        part.start()
    mate_kappa.start()
    send_all(faces)

    def arrange(first, values, keep):
        count = values.shape[0]
        if keep:
            rows_of[pl.ds(first, count), :] = values
        columns_of[:, pl.ds(first, count)] = values.T

    loaded.wait()
    inverse.start()
    arrange(pl.multiple_of(core * half, half), in_tiles(lambda ct: basis[ct, mine_x]), True)

    speeds.wait()
    own_kappa.wait()
    for k in range(3):
        speed[k] = (0.25 * jnp.broadcast_to(velocity[k:k + 1, :], (LANES, samples))).T

    all_in_from_ends()
    mate_back.wait_recv()
    mate_kappa.wait_recv()
    arrange(pl.multiple_of((1 - core) * half, half), in_tiles(lambda ct: basis[ct, theirs_x]), True)

    def rounded(rows, at):
        return dot(rows, columns_of[:, at], NN).astype(bf16).astype(f32)

    first_rows = jnp.concatenate([
        coefficients[CORES * peer(chip, e ^ far_x) + core, peer(me_n, d ^ far_n)].astype(bf16)
        for d in range(narrow) for e in range(chips)
    ], axis=0)
    inner = slice(0, cells)
    field[:, inner] = rounded(first_rows, inner)

    cell = lax.broadcasted_iota(jnp.int32, (1, cells), 1)
    y_of, z_of = (cell % pitch) // size_z, cell % size_z
    pick = (y_of == lax.broadcasted_iota(jnp.int32, (size_y, cells), 0)).astype(bf16)
    line = lax.broadcasted_iota(jnp.int32, (depth * size_z, cells), 0)
    own_row = (line == (cell // pitch) * size_z + z_of).astype(f32)
    rest = kappa[...].reshape(depth * size_z, size_y)
    found = jnp.zeros((depth * size_z, cells), f32)
    for _ in range(3):
        part = rest.astype(bf16)
        rest = rest - part.astype(f32)
        found = found + dot(part, pick, NN)
    factor[...] = jnp.broadcast_to(jnp.sum(found * own_row, axis=0, keepdims=True), factor.shape)

    all_in_go_on()
    take_all(edges)
    for k in range(edge_of.shape[0]):
        edge_of[k] = edge_in[k * LANES:(k + 1) * LANES, :].T.astype(f32)

    lane = lax.broadcasted_iota(jnp.int32, (8, LANES), 1)
    lane_x, lane_y, lane_z = lane // pitch, (lane % pitch) // size_z, lane % size_z
    per_tile = LANES // pitch
    low_y, high_y = lane_y == 0, lane_y == size_y - 1
    first_of_tile, last_of_tile = lane < pitch, lane >= LANES - pitch
    from_border = lane_x * size_z + lane_z + jnp.where(high_y, y_rows * size_z, 0)
    z_sign = jnp.where(lane_z == 0, 1.0, -1.0)

    def stencil(first, speeds_of, edge_rows):
        def at(t):
            if t >= tiles and edge_rows:
                return joined([edge_of[t - tiles, pl.ds(row, count), :] for row in edge_rows])
            return field[first:first + 8, t * LANES:(t + 1) * LANES]

        def turn(value, by):
            return pltpu.roll(value, by % LANES, 1)

        v_x, v_y, v_z = speeds_of
        if size_z == 2:
            v_z = v_z * z_sign
        center = [at(t) for t in range(tiles + 1)]
        ahead = [turn(value, -pitch) for value in center]
        behind = [turn(value, pitch) for value in center]
        y_border = at(tiles + 1)
        out = []
        for t in range(tiles):
            mid = center[t]
            x_next = jnp.where(last_of_tile, ahead[t + 1], ahead[t])
            x_prev = jnp.where(first_of_tile, behind[t - 1], behind[t])
            outside = jnp.take_along_axis(y_border, from_border + t * per_tile * size_z, axis=1)
            y_next = jnp.where(high_y, outside, turn(mid, -size_z))
            y_prev = jnp.where(low_y, outside, turn(mid, size_z))
            x_sum, y_sum = x_next + x_prev, y_next + y_prev
            carried = v_x * (x_sum * (x_next - x_prev)) + v_y * (y_sum * (y_next - y_prev))
            if size_z == 2:
                z_sum = jnp.where(lane_z == 0, turn(mid, -1), turn(mid, 1))
                carried = carried + v_z * (z_sum * z_sum)
            else:
                z_next = jnp.where(lane_z < size_z - 1, turn(mid, -1), 0.0)
                z_prev = jnp.where(lane_z > 0, turn(mid, 1), 0.0)
                z_sum = z_next + z_prev
                carried = carried + v_z * (z_sum * (z_next - z_prev))
            spread = x_sum + y_sum + z_sum - 6.0 * mid
            out.append(factor[:, t * LANES:(t + 1) * LANES] * spread - carried)
        return jnp.concatenate(out, axis=1)

    count = min(8, owned)

    def joined(pieces):
        return jnp.concatenate(pieces, axis=0) if len(pieces) > 1 else pieces[0]

    def places(first):
        for row in range(first, first + 8, count):
            d, e, inner = row // unit, row % unit // owned, row % owned
            x, n = peer(chip, e ^ far_x), peer(me_n, d ^ far_n)
            pair = (x * narrow + n) * owned + inner, ((CORES * x + core) * narrow + n) * owned + inner
            yield tuple(pl.multiple_of(at, 8) for at in pair) if count == 8 else pair

    def speeds_at(first):
        rows = [at for _, at in places(first)]
        return [joined([speed[k, pl.ds(at, count), :] for at in rows]) for k in range(3)]

    def slot(d, e):
        return d * chips + e - 1

    def scatter(group, step, residue):
        made = []
        for first in rows_in(group):
            edge_rows = [at for at, _ in places(first)] if step == 0 else []
            made.append(stencil(first, speeds_at(first), edge_rows))
        total = dot(jnp.concatenate(made, axis=0).astype(bf16), rows_of[...], NN)
        copies = []
        for i, (d, e) in enumerate(group):
            block = total[i * owned:(i + 1) * owned]
            if step == ITERS - 1 and d + e == 0 and far_n + far_x > 0:
                block = block + residue * (1.0 / (step_size * scale))
            to_n, to_x = (d ^ far_n, e ^ far_x) if step == ITERS - 1 else (d, e)
            if to_n + to_x == 0:
                kept[...] = block
                continue
            at = slot(to_n, to_x)
            reduced[at] = block.astype(WIRE)
            copies.append(remote(
                reduced.at[at], landed.at[step, at], r_send, r_recv[step],
                CORES * peer(chip, to_x) + core, peer(me_n, to_n),
            ))
        return copies

    def each(there):
        for d in range(narrow):
            for e in range(chips):
                if d + e > 0:
                    there(d, e)

    def reduced_sent():
        arrival(reduced, r_send, r_recv[0]).wait_send()

    def mine_sent():
        count = narrow * chips - 1 - (chips - 1 if relayed else 0)
        arrival(reduced.at[pl.ds(0, count)], g_send, r_recv[0]).wait_send()
        if relayed:
            arrival(reduced.at[pl.ds(0, chips - 1)], edge_send.at[2], r_recv[0]).wait_send()

    relayed = far_n > 0 and chips > 1
    blocks_of = [[(d, e) for e in reversed(range(chips))] for d in range(narrow)]
    nearer, farther = range(narrow // 2), range(narrow // 2, narrow)
    if owned % 8 == 0:
        far_first = [blocks_of[d] for d in reversed(farther)]
        far_first.append(sum((blocks_of[d] for d in reversed(nearer)), []))
        near_first = [[(0, 0)], [(0, e) for e in range(1, chips)]]
        near_first += [blocks_of[d][::-1] for d in nearer if d > 0]
        last = sum((blocks_of[d][::-1] for d in farther), [])
        late = [(d, e) for d, e in last if relayed and d == far_n and e > 0]
        near_first += [[block for block in last if block not in late], late]
        near_first = [group for group in near_first if group]
    else:
        far_first = [sum((blocks_of[d][::-1] for d in part), []) for part in (farther, nearer)]
        near_first = far_first[::-1]

    def rows_in(group):
        if owned % 8 == 0:
            return [(d * chips + e) * owned + inner for d, e in group for inner in range(0, owned, 8)]
        return range(group[0][0] * unit, (group[-1][0] + 1) * unit, 8)

    handing = max(4, narrow)
    state = coefficients[CORES * peer(chip, far_x) + core, peer(me_n, far_n)]
    residue = None
    for step in range(ITERS):
        if step > 0:
            reduced_sent()
        for number, group in enumerate(near_first if step else far_first):
            if step > 0:
                for d in sorted({d for d, e in group if d + e > 0}):
                    if relayed and d == far_n:
                        if (d, 0) in group:
                            arrival(gathered.at[d, 0], g_send, g_recv.at[d]).wait_recv()
                            for e in range(1, chips):
                                remote(
                                    gathered.at[d, 0], gathered.at[d, e], edge_send.at[2], g_recv.at[handing],
                                    CORES * peer(chip, e) + core, me_n,
                                ).start()
                        if (d, 1) in group:
                            arrival(gathered.at[d, pl.ds(1, chips - 1)], g_send, g_recv.at[handing]).wait_recv()
                    else:
                        beyond = gathered.at[d] if d > 0 else gathered.at[0, pl.ds(1, chips - 1)]
                        arrival(beyond, g_send, g_recv.at[d]).wait_recv()
                rows = jnp.concatenate([gathered[d, e] if d + e > 0 else mine[...] for d, e in group], axis=0)
                made = rounded(rows, slice(None))
                for i, (d, e) in enumerate(group):
                    at = (d * chips + e) * owned
                    field[at:at + owned, :] = made[i * owned:(i + 1) * owned]
            copies = scatter(group, step, residue)
            if step == 0 and number == 0:
                for pieces, sends, gone, comes in edges:
                    pl.when(sends)(gone.wait_send)
                all_in()
            for copy in copies:
                copy.start()

        if step == 0:
            take_all(faces)
            arrange(cells, in_tiles(lambda ct: border[ct]), False)
            inverse.wait()
            high = propagator[...].astype(bf16)
            g_high[...] = high.T
            g_low[...] = (propagator[...] - high.astype(f32)).astype(bf16).T

        arrival(landed.at[step], r_send, r_recv[step]).wait_recv()
        parts = [kept[...]]
        each(lambda d, e: parts.append(landed[step, slot(d, e)].astype(f32)))
        summed = sum(parts[1:], parts[0])

        if step == ITERS - 1 and far_n + far_x > 0:
            state = gathered[far_n, far_x].astype(f32)
        update = state + step_size * (summed * scale)
        high = update.astype(bf16)
        low = (update - high.astype(f32)).astype(bf16)
        both = dot(jnp.concatenate([high, low], axis=0), g_high[...], NN)
        small = both[owned:] + dot(high, g_low[...], NN)
        state = update + (both[:owned] + small)

        if step + 1 < ITERS:
            if step > 0:
                mine_sent()
            mine[...] = state.astype(bf16)
            residue = state - state.astype(bf16).astype(f32)
            for d in [*reversed(nearer), *reversed(farther)]:
                for e in reversed(range(chips)):
                    if d + e > 0 and not (relayed and d == far_n and e > 0):
                        remote(
                            mine, gathered.at[d, e], g_send, g_recv.at[d],
                            CORES * peer(chip, e) + core, peer(me_n, d),
                        ).start()

    out_ref[...] = state
    reduced_sent()
    mine_sent()
    for parts, sends, gone, comes in faces:
        pl.when(sends)(gone.wait_send)
    mate_gone.wait_send()
    mate_kappa.wait_send()


def body(basis, kappa, velocity, coefficients, propagator):
    size_x, size_y, size_z, modes = basis.shape
    samples = coefficients.shape[0]
    wide, narrow = lax.axis_size("wide"), lax.axis_size("narrow")
    chips = wide // CORES
    owned = samples // (wide * narrow)
    unit = chips * owned
    scale = 1.0 / math.sqrt(size_x * size_y * size_z * wide * narrow)
    pitch = size_y * size_z
    depth = CORES * size_x
    cells = depth * pitch
    assert LANES % pitch == 0 and cells % LANES == 0 and 2 * pitch <= LANES
    assert 2 * depth * size_z == LANES and unit % 8 == 0
    border = 2 * LANES // size_z
    dma = pltpu.SemaphoreType.DMA
    hbm = pl.BlockSpec(memory_space=pltpu.HBM)
    inputs = (
        basis, kappa.transpose(0, 2, 1), velocity,
        coefficients.reshape(wide, narrow, owned, modes), propagator,
    )
    return pl.pallas_call(
        functools.partial(kernel, chips, narrow, scale),
        out_shape=jax.ShapeDtypeStruct((owned, modes), f32),
        in_specs=[hbm] * len(inputs),
        out_specs=pl.BlockSpec(memory_space=pltpu.VMEM),
        scratch_shapes=[
            pltpu.VMEM((modes // LANES, depth, size_y, size_z, LANES), bf16),
            pltpu.VMEM((modes // LANES, border, size_z, LANES), bf16),
            pltpu.VMEM((CORES, size_x, size_z, size_y), f32),
            pltpu.VMEM((3, samples), f32),
            pltpu.VMEM((wide, narrow, owned, modes), f32),
            pltpu.VMEM((modes, modes), f32),
            pltpu.VMEM((modes // LANES, 2 * size_x + size_y, size_z, LANES), bf16),
            pltpu.VMEM((CORES, (2 * size_x + size_y) * size_z, narrow * unit), bf16),
            pltpu.VMEM((border * size_z, narrow * unit), bf16),
            pltpu.VMEM((border * size_z // LANES, narrow * unit, LANES), f32),
            pltpu.VMEM((cells, modes), bf16),
            pltpu.VMEM((modes, cells + border * size_z), bf16),
            pltpu.VMEM((narrow * unit, cells + border * size_z), f32),
            pltpu.VMEM((8, cells), f32),
            pltpu.VMEM((3, samples, LANES), f32),
            pltpu.VMEM((modes, modes), bf16),
            pltpu.VMEM((modes, modes), bf16),
            pltpu.VMEM((narrow * chips - 1, owned, modes), WIRE),
            pltpu.VMEM((ITERS, narrow * chips - 1, owned, modes), WIRE),
            pltpu.VMEM((owned, modes), f32),
            pltpu.VMEM((owned, modes), bf16),
            pltpu.VMEM((narrow, chips, owned, modes), bf16),
            dma((5,)), dma((2,)), dma((4,)), dma((5,)), dma, dma((3,)), dma((max(4, narrow) + 1,)),
            pltpu.SemaphoreType.REGULAR((4 if chips > 2 else 2,)),
        ],
        compiler_params=pltpu.CompilerParams(
            collective_id=0, has_side_effects=True, vmem_limit_bytes=48 * 1024 * 1024
        ),
    )(*(pltpu.with_memory_space_constraint(value, pltpu.HBM) for value in inputs))


def solution(mesh):
    placed = (
        P(("groups", "wide"), "narrow", None, None),
        P(("groups", "wide"), "narrow", None),
        P(None, "groups"),
        P("groups", None),
        P("groups", None),
    )
    return jax.shard_map(
        body,
        mesh=mesh,
        in_specs=placed,
        out_specs=P(("groups", "wide", "narrow"), None),
        check_vma=False,
    )
```

```python
import functools
import math

import jax
import jax.numpy as jnp
from jax import lax
from jax.experimental import pallas as pl
from jax.experimental.pallas import tpu as pltpu
from jax.sharding import PartitionSpec as P

ITERS = 2
WIRE = jnp.bfloat16
LANES = 128
CORES = 2

step_size = 4.0

NT = (((1,), (1,)), ((), ()))
NN = (((1,), (0,)), ((), ()))
f32, bf16 = jnp.float32, jnp.bfloat16


def peer(me, offset):
    result, bit = me, 1
    while bit <= offset:
        if offset & bit:
            result = result + (1 - 2 * ((me // bit) % 2)) * bit
        bit *= 2
    return result


def dot(a, b, dims):
    return lax.dot_general(a, b, dims, preferred_element_type=f32)


def kernel(
    chips, narrow, scale,
    basis_hbm, kappa_hbm, velocity_hbm, coefficients_hbm, propagator_hbm, out_ref,
    basis, border, kappa, velocity, coefficients, propagator,
    own_rows, edge_out, edge_in, edge_of, rows_of, columns_of, field, factor, speed, g_high, g_low,
    reduced, landed, kept, mine, gathered,
    load_sem, mate_recv, face_recv, out_send,
    first_recv, edge_send, edge_recv, word,
):
    r_send, g_send, g_recv = edge_send.at[0], edge_send.at[1], edge_recv
    r_recv = [first_recv] + [mate_recv.at[k] for k in range(ITERS - 1)]
    size_x, size_y, size_z, modes = basis_hbm.shape
    slices, depth = basis.shape[:2]
    owned = coefficients.shape[2]
    samples = velocity.shape[1]
    unit = chips * owned
    pitch = size_y * size_z
    half, cells = size_x * pitch, depth * pitch
    tiles = cells // LANES
    x_rows, y_rows = size_y, depth
    y_base = border.shape[1] - 2 * y_rows
    x_base = (y_base - x_rows, 0)
    wide = chips * CORES
    me_w, me_n = lax.axis_index("wide"), lax.axis_index("narrow")
    chip, core = me_w // CORES, me_w % CORES
    far_x, far_n = chips // 2, narrow // 2

    def lanes_of(ct):
        return pl.ds(ct * LANES, LANES)

    mine_x, theirs_x = pl.ds(core * size_x, size_x), pl.ds((1 - core) * size_x, size_x)
    started = pltpu.make_async_copy(coefficients_hbm, coefficients, load_sem.at[3])
    started.start()
    outer_rows = pltpu.make_async_copy(own_rows, own_rows, load_sem.at[2])
    for ct in range(slices):
        for first, count, face in (
            (0, size_x, basis_hbm.at[:, size_y - 1, :, lanes_of(ct)]),
            (size_x, size_x, basis_hbm.at[:, 0, :, lanes_of(ct)]),
            (2 * size_x, size_y, basis_hbm.at[core * (size_x - 1), :, :, lanes_of(ct)]),
        ):
            pltpu.make_async_copy(face, own_rows.at[ct, pl.ds(first, count)], load_sem.at[2]).start()
    loads = [
        pltpu.make_async_copy(basis_hbm.at[:, :, :, lanes_of(ct)], basis.at[ct, mine_x], load_sem.at[0])
        for ct in range(slices)
    ]
    loaded = pltpu.make_async_copy(basis.at[:, mine_x], basis.at[:, mine_x], load_sem.at[0])
    for load in loads:
        load.start()
    own_kappa = pltpu.make_async_copy(kappa_hbm, kappa.at[core], load_sem.at[1])
    own_kappa.start()
    speeds = pltpu.make_async_copy(velocity_hbm, velocity, load_sem.at[4])
    speeds.start()
    inverse = pltpu.make_async_copy(propagator_hbm, propagator, load_sem.at[3])


    barrier = pltpu.get_barrier_semaphore()

    def greet(w, n):
        pl.semaphore_signal(
            barrier, inc=1, device_id={"wide": w, "narrow": n}, device_id_type=pl.DeviceIdType.MESH
        )

    greet(peer(me_w, 1), me_n)
    greetings = 1
    for step in (-1, 1):
        n, x = me_n + step, chip + step
        n_there = jnp.logical_and(n >= 0, n < narrow)
        x_there = jnp.logical_and(x >= 0, x < chips)

        def along_narrow(n=n):
            for k in range(CORES):
                greet(peer(me_w, k), n)

        def along_wide(x=x):
            for k in range(CORES):
                greet(CORES * x + k, me_n)

        pl.when(n_there)(along_narrow)
        pl.when(x_there)(along_wide)
        greetings = greetings + CORES * (jnp.where(n_there, 1, 0) + jnp.where(x_there, 1, 0))

    def clear(first, count):
        border[:, pl.ds(first, count)] = jnp.zeros((slices, count) + border.shape[2:], bf16)
        at = slice(first * size_z, (first + count) * size_z)
        edge_in[at, :] = jnp.zeros((count * size_z, edge_in.shape[1]), bf16)

    pl.when(chip == 0)(lambda: clear(x_base[0], x_rows))
    pl.when(chip == chips - 1)(lambda: clear(x_base[1], x_rows))
    pl.when(me_n == 0)(lambda: clear(y_base, y_rows))
    pl.when(me_n == narrow - 1)(lambda: clear(y_base + y_rows, y_rows))

    pl.semaphore_wait(barrier, greetings)

    def lines(count, at, where, forth, back):
        def tell(sem, step):
            pl.semaphore_signal(
                sem, inc=1, device_id=where(at + step), device_id_type=pl.DeviceIdType.MESH
            )

        def begin():
            pl.when(at == 0)(lambda: tell(forth, 1))
            pl.when(at == count - 1)(lambda: tell(back, -1))

        def pass_on(sem, step):
            pl.semaphore_wait(sem, 1)
            tell(sem, step)

        def from_ends():
            if count > 2:
                pl.when(at == 1)(lambda: pass_on(forth, 1))
                pl.when(at == count - 2)(lambda: pass_on(back, -1))

        def go_on():
            if count > 3:
                pl.when(jnp.logical_and(at > 1, at < count - 1))(lambda: pass_on(forth, 1))
                pl.when(jnp.logical_and(at > 0, at < count - 2))(lambda: pass_on(back, -1))

        def end():
            pl.when(at == count - 1)(lambda: pl.semaphore_wait(forth, 1))
            pl.when(at == 0)(lambda: pl.semaphore_wait(back, 1))

        return begin, from_ends, go_on, end

    if chips > 2:
        for phase in lines(
            chips, chip, lambda x: {"wide": CORES * x + core, "narrow": me_n}, word.at[2], word.at[3]
        ):
            phase()
    all_in_begin, all_in_from_ends, all_in_go_on, all_in = lines(
        narrow, me_n, lambda n: {"wide": me_w, "narrow": n}, word.at[0], word.at[1]
    )
    all_in_begin()

    def remote(src, dst, send, recv, w, n):
        return pltpu.make_async_remote_copy(
            src_ref=src, dst_ref=dst, send_sem=send, recv_sem=recv,
            device_id={"wide": w, "narrow": n}, device_id_type=pl.DeviceIdType.MESH,
        )

    def arrival(ref, send, recv):
        return remote(ref, ref, send, recv, me_w, me_n)

    faces, edges = [], []
    line_x, line_y = size_y * size_z, size_x * size_z

    def edge(face, first, count, number, came, w, n):
        parts = [
            remote(
                edge_out.at[k, pl.ds(face[0], face[1])], edge_in.at[pl.ds(first, count)],
                edge_send.at[number], edge_recv.at[came], w(k), n,
            )
            for k in range(CORES)
        ]
        gone = arrival(edge_in.at[pl.ds(0, CORES * count)], edge_send.at[number], edge_recv.at[came])
        return parts, gone

    def whole_edge(first, count, number):
        return arrival(edge_in.at[pl.ds(first * size_z, count * size_z)], edge_send.at[0], edge_recv.at[number])

    for j, (from_y, step) in enumerate(((size_y - 1, 1), (0, -1))):
        n = lax.rem(me_n + step + narrow, narrow)
        first = y_base + j * y_rows
        parts = [
            remote(
                basis_hbm.at[:, from_y, :, lanes_of(ct)], border.at[ct, pl.ds(first + core * size_x, size_x)],
                out_send.at[j], face_recv.at[j], peer(me_w, k), n,
            )
            for k in range(CORES) for ct in range(slices)
        ]
        came = arrival(border.at[:, pl.ds(first, y_rows)], out_send.at[j], face_recv.at[j])
        goes = jnp.logical_and(me_n + step >= 0, me_n + step < narrow)
        there = jnp.logical_and(me_n - step >= 0, me_n - step < narrow)
        faces.append((parts, goes, came, [(came, there)]))
        at = pl.multiple_of(first * size_z + core * line_y, line_y)
        parts, gone = edge((j * line_y, line_y), at, line_y, j, j, lambda k: CORES * chip + k, n)
        edges.append((parts, goes, gone, [(whole_edge(first, y_rows, j), there)]))
    toward = chip + 2 * core - 1
    x_to = lax.rem(toward + chips, chips)
    parts = [
        remote(
            basis_hbm.at[core * (size_x - 1), :, :, lanes_of(ct)], border.at[ct, pl.ds(core * x_base[0], x_rows)],
            out_send.at[2], face_recv.at[2 + core], CORES * x_to + k, me_n,
        )
        for k in range(CORES) for ct in range(slices)
    ]
    goes = jnp.logical_and(toward >= 0, toward < chips)
    faces.append((
        parts, goes,
        arrival(border.at[:, pl.ds(0, CORES * x_rows)], out_send.at[2], face_recv.at[2]),
        [
            (arrival(border.at[:, pl.ds(k * x_base[0], x_rows)], out_send.at[2], face_recv.at[2 + k]), there)
            for k, there in ((0, chip < chips - 1), (1, chip > 0))
        ],
    ))
    at = pl.multiple_of(core * (x_base[0] * size_z), line_x)
    parts, gone = edge((2 * line_y, line_x), at, line_x, 2, 2 + core, lambda k: CORES * x_to + k, me_n)
    edges.append((parts, goes, gone, [
        (whole_edge(k * x_base[0], x_rows, 2 + k), there) for k, there in ((0, chip < chips - 1), (1, chip > 0))
    ]))

    def send_all(copies):
        for parts, sends, gone, comes in copies:
            def go(parts=parts):
                for part in parts:
                    part.start()
            pl.when(sends)(go)

    def take_all(copies):
        for parts, sends, gone, comes in copies:
            for came, there in comes:
                pl.when(there)(came.wait_recv)

    mate = [
        remote(
            basis_hbm.at[:, :, :, lanes_of(ct)], basis.at[ct, mine_x],
            out_send.at[3], mate_recv.at[0], peer(me_w, 1), me_n,
        )
        for ct in range(slices)
    ]
    mate_gone = arrival(basis.at[:, mine_x], out_send.at[3], mate_recv.at[0])
    mate_back = arrival(basis.at[:, theirs_x], out_send.at[3], mate_recv.at[0])
    mate_kappa = remote(kappa_hbm, kappa.at[core], out_send.at[4], mate_recv.at[1], peer(me_w, 1), me_n)

    started.wait()
    outer_rows.wait()

    def in_tiles(of):
        return jnp.concatenate([of(ct).reshape(-1, LANES) for ct in range(slices)], axis=1)

    own_edge = in_tiles(lambda ct: own_rows[ct])
    those = jnp.concatenate([
        coefficients[CORES * x + k].reshape(narrow * owned, modes).astype(bf16)
        for k in range(CORES) for x in range(chips)
    ], axis=0)
    on_edge = dot(own_edge, those, NT).astype(bf16)
    for k in range(CORES):
        edge_out[k] = on_edge[:, k * narrow * unit:(k + 1) * narrow * unit]
    send_all(edges)
    for part in mate:
        part.start()
    mate_kappa.start()
    send_all(faces)

    def arrange(first, values, keep):
        count = values.shape[0]
        if keep:
            rows_of[pl.ds(first, count), :] = values
        columns_of[:, pl.ds(first, count)] = values.T

    loaded.wait()
    inverse.start()
    arrange(pl.multiple_of(core * half, half), in_tiles(lambda ct: basis[ct, mine_x]), True)

    speeds.wait()
    own_kappa.wait()
    for k in range(3):
        speed[k] = (0.25 * jnp.broadcast_to(velocity[k:k + 1, :], (LANES, samples))).T

    all_in_from_ends()
    mate_back.wait_recv()
    mate_kappa.wait_recv()
    arrange(pl.multiple_of((1 - core) * half, half), in_tiles(lambda ct: basis[ct, theirs_x]), True)

    def rounded(rows, at):
        return dot(rows, columns_of[:, at], NN).astype(bf16).astype(f32)

    first_rows = jnp.concatenate([
        coefficients[CORES * peer(chip, e ^ far_x) + core, peer(me_n, d ^ far_n)].astype(bf16)
        for d in range(narrow) for e in range(chips)
    ], axis=0)
    inner = slice(0, cells)
    field[:, inner] = rounded(first_rows, inner)

    cell = lax.broadcasted_iota(jnp.int32, (1, cells), 1)
    y_of, z_of = (cell % pitch) // size_z, cell % size_z
    pick = (y_of == lax.broadcasted_iota(jnp.int32, (size_y, cells), 0)).astype(bf16)
    line = lax.broadcasted_iota(jnp.int32, (depth * size_z, cells), 0)
    own_row = (line == (cell // pitch) * size_z + z_of).astype(f32)
    rest = kappa[...].reshape(depth * size_z, size_y)
    found = jnp.zeros((depth * size_z, cells), f32)
    for _ in range(3):
        part = rest.astype(bf16)
        rest = rest - part.astype(f32)
        found = found + dot(part, pick, NN)
    factor[...] = jnp.broadcast_to(jnp.sum(found * own_row, axis=0, keepdims=True), factor.shape)

    all_in_go_on()
    take_all(edges)
    for k in range(edge_of.shape[0]):
        edge_of[k] = edge_in[k * LANES:(k + 1) * LANES, :].T.astype(f32)

    lane = lax.broadcasted_iota(jnp.int32, (8, LANES), 1)
    lane_x, lane_y, lane_z = lane // pitch, (lane % pitch) // size_z, lane % size_z
    per_tile = LANES // pitch
    low_y, high_y = lane_y == 0, lane_y == size_y - 1
    first_of_tile, last_of_tile = lane < pitch, lane >= LANES - pitch
    from_border = lane_x * size_z + lane_z + jnp.where(high_y, y_rows * size_z, 0)
    z_sign = jnp.where(lane_z == 0, 1.0, -1.0)

    def stencil(first, speeds_of, edge_rows):
        def at(t):
            if t >= tiles and edge_rows:
                return joined([edge_of[t - tiles, pl.ds(row, count), :] for row in edge_rows])
            return field[first:first + 8, t * LANES:(t + 1) * LANES]

        def turn(value, by):
            return pltpu.roll(value, by % LANES, 1)

        v_x, v_y, v_z = speeds_of
        if size_z == 2:
            v_z = v_z * z_sign
        center = [at(t) for t in range(tiles + 1)]
        ahead = [turn(value, -pitch) for value in center]
        behind = [turn(value, pitch) for value in center]
        y_border = at(tiles + 1)
        out = []
        for t in range(tiles):
            mid = center[t]
            x_next = jnp.where(last_of_tile, ahead[t + 1], ahead[t])
            x_prev = jnp.where(first_of_tile, behind[t - 1], behind[t])
            outside = jnp.take_along_axis(y_border, from_border + t * per_tile * size_z, axis=1)
            y_next = jnp.where(high_y, outside, turn(mid, -size_z))
            y_prev = jnp.where(low_y, outside, turn(mid, size_z))
            x_sum, y_sum = x_next + x_prev, y_next + y_prev
            carried = v_x * (x_sum * (x_next - x_prev)) + v_y * (y_sum * (y_next - y_prev))
            if size_z == 2:
                z_sum = jnp.where(lane_z == 0, turn(mid, -1), turn(mid, 1))
                carried = carried + v_z * (z_sum * z_sum)
            else:
                z_next = jnp.where(lane_z < size_z - 1, turn(mid, -1), 0.0)
                z_prev = jnp.where(lane_z > 0, turn(mid, 1), 0.0)
                z_sum = z_next + z_prev
                carried = carried + v_z * (z_sum * (z_next - z_prev))
            spread = x_sum + y_sum + z_sum - 6.0 * mid
            out.append(factor[:, t * LANES:(t + 1) * LANES] * spread - carried)
        return jnp.concatenate(out, axis=1)

    count = min(8, owned)

    def joined(pieces):
        return jnp.concatenate(pieces, axis=0) if len(pieces) > 1 else pieces[0]

    def places(first):
        for row in range(first, first + 8, count):
            d, e, inner = row // unit, row % unit // owned, row % owned
            x, n = peer(chip, e ^ far_x), peer(me_n, d ^ far_n)
            pair = (x * narrow + n) * owned + inner, ((CORES * x + core) * narrow + n) * owned + inner
            yield tuple(pl.multiple_of(at, 8) for at in pair) if count == 8 else pair

    def speeds_at(first):
        rows = [at for _, at in places(first)]
        return [joined([speed[k, pl.ds(at, count), :] for at in rows]) for k in range(3)]

    def slot(d, e):
        return d * chips + e - 1

    def scatter(group, step, residue):
        made = []
        for first in rows_in(group):
            edge_rows = [at for at, _ in places(first)] if step == 0 else []
            made.append(stencil(first, speeds_at(first), edge_rows))
        total = dot(jnp.concatenate(made, axis=0).astype(bf16), rows_of[...], NN)
        copies = []
        for i, (d, e) in enumerate(group):
            block = total[i * owned:(i + 1) * owned]
            if step == ITERS - 1 and d + e == 0 and far_n + far_x > 0:
                block = block + residue * (1.0 / (step_size * scale))
            to_n, to_x = (d ^ far_n, e ^ far_x) if step == ITERS - 1 else (d, e)
            if to_n + to_x == 0:
                kept[...] = block
                continue
            at = slot(to_n, to_x)
            reduced[at] = block.astype(WIRE)
            copies.append(remote(
                reduced.at[at], landed.at[step, at], r_send, r_recv[step],
                CORES * peer(chip, to_x) + core, peer(me_n, to_n),
            ))
        return copies

    def each(there):
        for d in range(narrow):
            for e in range(chips):
                if d + e > 0:
                    there(d, e)

    def reduced_sent():
        arrival(reduced, r_send, r_recv[0]).wait_send()

    def mine_sent():
        count = narrow * chips - 1 - (chips - 1 if relayed else 0)
        arrival(reduced.at[pl.ds(0, count)], g_send, r_recv[0]).wait_send()
        if relayed:
            arrival(reduced.at[pl.ds(0, chips - 1)], edge_send.at[2], r_recv[0]).wait_send()

    relayed = far_n > 0 and chips > 1
    blocks_of = [[(d, e) for e in reversed(range(chips))] for d in range(narrow)]
    nearer, farther = range(narrow // 2), range(narrow // 2, narrow)
    if owned % 8 == 0:
        far_first = [blocks_of[narrow - 1], sum((blocks_of[d] for d in range(narrow - 2, 0, -1)), []), blocks_of[0]]
        far_first = [group for group in far_first if group]
        near_first = [[(0, 0)], [(0, e) for e in range(1, chips)]]
        near_first += [blocks_of[d][::-1] for d in nearer if d > 0]
        last = sum((blocks_of[d][::-1] for d in farther), [])
        late = [(d, e) for d, e in last if relayed and d == far_n and e > 0]
        near_first += [[block for block in last if block not in late], late]
        near_first = [group for group in near_first if group]
    else:
        far_first = [sum((blocks_of[d][::-1] for d in part), []) for part in (farther, nearer)]
        near_first = far_first[::-1]

    def rows_in(group):
        if owned % 8 == 0:
            return [(d * chips + e) * owned + inner for d, e in group for inner in range(0, owned, 8)]
        return range(group[0][0] * unit, (group[-1][0] + 1) * unit, 8)

    handing = max(4, narrow)
    state = coefficients[CORES * peer(chip, far_x) + core, peer(me_n, far_n)]
    residue = None
    for step in range(ITERS):
        if step > 0:
            reduced_sent()
        for number, group in enumerate(near_first if step else far_first):
            if step > 0:
                for d in sorted({d for d, e in group if d + e > 0}):
                    if relayed and d == far_n:
                        if (d, 0) in group:
                            arrival(gathered.at[d, 0], g_send, g_recv.at[d]).wait_recv()
                            for e in range(1, chips):
                                remote(
                                    gathered.at[d, 0], gathered.at[d, e], edge_send.at[2], g_recv.at[handing],
                                    CORES * peer(chip, e) + core, me_n,
                                ).start()
                        if (d, 1) in group:
                            arrival(gathered.at[d, pl.ds(1, chips - 1)], g_send, g_recv.at[handing]).wait_recv()
                    else:
                        beyond = gathered.at[d] if d > 0 else gathered.at[0, pl.ds(1, chips - 1)]
                        arrival(beyond, g_send, g_recv.at[d]).wait_recv()
                rows = jnp.concatenate([gathered[d, e] if d + e > 0 else mine[...] for d, e in group], axis=0)
                made = rounded(rows, slice(None))
                for i, (d, e) in enumerate(group):
                    at = (d * chips + e) * owned
                    field[at:at + owned, :] = made[i * owned:(i + 1) * owned]
            copies = scatter(group, step, residue)
            if step == 0 and number == 0:
                for pieces, sends, gone, comes in edges:
                    pl.when(sends)(gone.wait_send)
                all_in()
            for copy in copies:
                copy.start()

        if step == 0:
            take_all(faces)
            arrange(cells, in_tiles(lambda ct: border[ct]), False)
            inverse.wait()
            high = propagator[...].astype(bf16)
            g_high[...] = high.T
            g_low[...] = (propagator[...] - high.astype(f32)).astype(bf16).T

        arrival(landed.at[step], r_send, r_recv[step]).wait_recv()
        parts = [kept[...]]
        each(lambda d, e: parts.append(landed[step, slot(d, e)].astype(f32)))
        summed = sum(parts[1:], parts[0])

        if step == ITERS - 1 and far_n + far_x > 0:
            state = gathered[far_n, far_x].astype(f32)
        update = state + step_size * (summed * scale)
        high = update.astype(bf16)
        low = (update - high.astype(f32)).astype(bf16)
        both = dot(jnp.concatenate([high, low], axis=0), g_high[...], NN)
        small = both[owned:] + dot(high, g_low[...], NN)
        state = update + (both[:owned] + small)

        if step + 1 < ITERS:
            if step > 0:
                mine_sent()
            mine[...] = state.astype(bf16)
            residue = state - state.astype(bf16).astype(f32)
            for d in [*reversed(nearer), *reversed(farther)]:
                for e in reversed(range(chips)):
                    if d + e > 0 and not (relayed and d == far_n and e > 0):
                        remote(
                            mine, gathered.at[d, e], g_send, g_recv.at[d],
                            CORES * peer(chip, e) + core, peer(me_n, d),
                        ).start()

    out_ref[...] = state
    reduced_sent()
    mine_sent()
    for parts, sends, gone, comes in faces:
        pl.when(sends)(gone.wait_send)
    mate_gone.wait_send()
    mate_kappa.wait_send()


def body(basis, kappa, velocity, coefficients, propagator):
    size_x, size_y, size_z, modes = basis.shape
    samples = coefficients.shape[0]
    wide, narrow = lax.axis_size("wide"), lax.axis_size("narrow")
    chips = wide // CORES
    owned = samples // (wide * narrow)
    unit = chips * owned
    scale = 1.0 / math.sqrt(size_x * size_y * size_z * wide * narrow)
    pitch = size_y * size_z
    depth = CORES * size_x
    cells = depth * pitch
    assert LANES % pitch == 0 and cells % LANES == 0 and 2 * pitch <= LANES
    assert 2 * depth * size_z == LANES and unit % 8 == 0
    border = 2 * LANES // size_z
    dma = pltpu.SemaphoreType.DMA
    hbm = pl.BlockSpec(memory_space=pltpu.HBM)
    inputs = (
        basis, kappa.transpose(0, 2, 1), velocity,
        coefficients.reshape(wide, narrow, owned, modes), propagator,
    )
    return pl.pallas_call(
        functools.partial(kernel, chips, narrow, scale),
        out_shape=jax.ShapeDtypeStruct((owned, modes), f32),
        in_specs=[hbm] * len(inputs),
        out_specs=pl.BlockSpec(memory_space=pltpu.VMEM),
        scratch_shapes=[
            pltpu.VMEM((modes // LANES, depth, size_y, size_z, LANES), bf16),
            pltpu.VMEM((modes // LANES, border, size_z, LANES), bf16),
            pltpu.VMEM((CORES, size_x, size_z, size_y), f32),
            pltpu.VMEM((3, samples), f32),
            pltpu.VMEM((wide, narrow, owned, modes), f32),
            pltpu.VMEM((modes, modes), f32),
            pltpu.VMEM((modes // LANES, 2 * size_x + size_y, size_z, LANES), bf16),
            pltpu.VMEM((CORES, (2 * size_x + size_y) * size_z, narrow * unit), bf16),
            pltpu.VMEM((border * size_z, narrow * unit), bf16),
            pltpu.VMEM((border * size_z // LANES, narrow * unit, LANES), f32),
            pltpu.VMEM((cells, modes), bf16),
            pltpu.VMEM((modes, cells + border * size_z), bf16),
            pltpu.VMEM((narrow * unit, cells + border * size_z), f32),
            pltpu.VMEM((8, cells), f32),
            pltpu.VMEM((3, samples, LANES), f32),
            pltpu.VMEM((modes, modes), bf16),
            pltpu.VMEM((modes, modes), bf16),
            pltpu.VMEM((narrow * chips - 1, owned, modes), WIRE),
            pltpu.VMEM((ITERS, narrow * chips - 1, owned, modes), WIRE),
            pltpu.VMEM((owned, modes), f32),
            pltpu.VMEM((owned, modes), bf16),
            pltpu.VMEM((narrow, chips, owned, modes), bf16),
            dma((5,)), dma((2,)), dma((4,)), dma((5,)), dma, dma((3,)), dma((max(4, narrow) + 1,)),
            pltpu.SemaphoreType.REGULAR((4 if chips > 2 else 2,)),
        ],
        compiler_params=pltpu.CompilerParams(
            collective_id=0, has_side_effects=True, vmem_limit_bytes=48 * 1024 * 1024
        ),
    )(*(pltpu.with_memory_space_constraint(value, pltpu.HBM) for value in inputs))


def solution(mesh):
    placed = (
        P(("groups", "wide"), "narrow", None, None),
        P(("groups", "wide"), "narrow", None),
        P(None, "groups"),
        P("groups", None),
        P("groups", None),
    )
    return jax.shard_map(
        body,
        mesh=mesh,
        in_specs=placed,
        out_specs=P(("groups", "wide", "narrow"), None),
        check_vma=False,
    )
```
